512 devices in a mesh: dp: 32 (over x, y), seq: 16 (over z, core).
Axes of the slice: x: 4, y: 8, z: 8, core: 2. Of those that a mesh axis runs over, the one named last changes fastest.
Arguments:
- features: bfloat16 [32, 2048, 2560], P('dp', 'seq'), may hold values from -6 to 6
- head_inputs: bfloat16 [32, 2048, 2560], P('dp', 'seq'), may hold values from -6 to 6
- out_grad: bfloat16 [32, 2048, 2560], P('dp', 'seq'), may hold values from -6 to 6
- bc_weight: bfloat16 [2560, 128], P('dp'), may hold values from -0.125 to 0.125
- dt_weight: bfloat16 [2560, 40], P('dp'), may hold values from -0.125 to 0.125
- dt_bias: float32 [40], replicated, may hold values from -7 to -5.5
- decay_rate: float32 [40], replicated, may hold values from 0.078125 to 16
- skip_gain: float32 [40], replicated, may hold values from 0.5 to 1.5
Outputs:
- input_grad: bfloat16 [32, 2048, 2560], P('dp', 'seq')
- head_grad: bfloat16 [32, 2048, 2560], P('dp', 'seq')
- bc_weight_grad: float32 [2560, 128], P('dp')
- dt_weight_grad: float32 [2560, 40], P('dp')
The draws below stay inside these ranges and needn't reach their ends.
All inputs are finite; a program needn't handle non-finite values.
Results may differ from the reference program's by a relative error of at most 0.0049.
Values may be sent and summed in bfloat16 or wider, within the bound.
No kernel may reach another device: no remote copies, remote signals or barrier semaphores. Data moves between devices by JAX's collectives and lax.ppermute only.
A program may use at most 128 MiB of HBM per device.

```python
import math
from functools import partial
import jax
import jax.numpy as jnp
from jax import lax

D = 2560
HEADS = 40
HEAD_DIM = 64
STATE = 64
TOK_DEV = 128
STREAMS = 32
SEQ_LEN = 2048
INNER = 2560


def spiked(drawn, key, source, target, shards_of, factor):
    def block_of(dim):
        return (jnp.arange(drawn.shape[dim]) // (drawn.shape[dim] // shards_of)).reshape((-1,) + (1,) * (drawn.ndim - 1 - dim))

    near = jax.random.permutation(key, shards_of)[block_of(target)]
    second = (block_of(target) + shards_of // 2) % shards_of
    return jnp.where((block_of(source) == near) | (block_of(source) == second), factor * drawn, drawn)


def block_scale(rng, shape, shards, least, largest):
    factor_of, own = 1.0, jax.random.fold_in(rng, 6)
    for position, parts in shards:
        steps = jnp.exp(jax.random.uniform(jax.random.fold_in(own, position), (parts,), jnp.float32, least / len(shards), largest / len(shards)))
        factor_of = factor_of * jnp.repeat(steps, shape[position] // parts).reshape([-1 if axis == position else 1 for axis in range(len(shape))])
    return factor_of


def bell_draw(own_key, dims, spread, most, split=(), held_as=jnp.bfloat16):
    array = spread * jax.random.normal(own_key, dims, jnp.float32)
    if split:
        array = array * block_scale(own_key, dims, split, -0.22, 0.18)
    return jnp.clip(array, -most, most).astype(held_as)


def bell_draw_with(key, dims, width, limit, split, heavy, kind=jnp.bfloat16):
    entries = width * jax.random.normal(key, dims, jnp.float32)
    if split:
        entries = entries * block_scale(key, dims, split, -0.22, 0.18)
    return jnp.clip(spiked(entries, jax.random.fold_in(key, 3), *heavy), -limit, limit).astype(kind)


def setup_inputs(seed: int = 0) -> dict:
    seeds = jax.random.split(jax.random.key(seed), 9)
    features = bell_draw_with(seeds[0], (STREAMS, SEQ_LEN, D), 1.0, 6.0, ((0, 32), (1, 16)), (0, 2, 32, 2.75))
    head_inputs = bell_draw(seeds[1], (STREAMS, SEQ_LEN, INNER), 1.0, 6.0, ((0, 32), (1, 16)))
    out_grad = bell_draw(seeds[2], (STREAMS, SEQ_LEN, INNER), 1.0, 6.0, ((0, 32), (1, 16)))
    bc_weight = bell_draw(seeds[3], (D, 2 * STATE), D ** -0.5, 0.125, ((0, 32),))
    dt_weight = bell_draw(seeds[4], (D, HEADS), D ** -0.5, 0.125, ((0, 32),))
    dt_bias = jnp.clip(jax.random.uniform(seeds[5], (HEADS,), jnp.float32, -7.0, -5.5), -7.0, -5.5)
    decay_rate = jnp.clip(jnp.exp(jax.random.uniform(seeds[6], (HEADS,), jnp.float32, math.log(0.078125), math.log(16.0))), 0.078125, 16.0)
    skip_gain = jnp.clip(jax.random.uniform(seeds[7], (HEADS,), jnp.float32, 0.5, 1.5), 0.5, 1.5)
    return dict(features=features, head_inputs=head_inputs, out_grad=out_grad, bc_weight=bc_weight, dt_weight=dt_weight, dt_bias=dt_bias, decay_rate=decay_rate, skip_gain=skip_gain)


highest = lax.Precision.HIGHEST

def spread_heads(values, head_size):
    return jnp.repeat(values, head_size, axis=-1)

def block_pass(decay_rate, skip_gain, carry_state, block):
    inputs_f, step_size, b_rows, c_rows = block
    length = inputs_f.shape[0]
    log_decay = -decay_rate[None, :] * step_size
    cumulative = jnp.cumsum(log_decay, axis=0)
    total_decay = cumulative[-1]
    scaled_in = inputs_f * spread_heads(step_size, HEAD_DIM)
    positions = jnp.arange(length)
    causal = positions[:, None] >= positions[None, :]
    gap = cumulative.T[:, :, None] - cumulative.T[:, None, :]
    weights_mat = jnp.exp(jnp.where(causal[None], gap, -1e+30))
    intersection = jnp.dot(c_rows, b_rows.T, precision=highest)
    mixing = intersection[None] * weights_mat
    inner_out = jnp.einsum('htu,uhp->thp', mixing, scaled_in.reshape(length, HEADS, HEAD_DIM), precision=highest)
    inner_out = inner_out.reshape(length, INNER)
    carried_out = jnp.dot(c_rows, carry_state, precision=highest) * spread_heads(jnp.exp(cumulative), HEAD_DIM)
    output = inner_out + carried_out + inputs_f * spread_heads(skip_gain, HEAD_DIM)[None, :]
    to_end = spread_heads(jnp.exp(total_decay[None, :] - cumulative), HEAD_DIM)
    local_state = jnp.dot(b_rows.T, scaled_in * to_end, precision=highest)
    new_state = carry_state * spread_heads(jnp.exp(total_decay), HEAD_DIM)[None, :] + local_state
    return (new_state, output)

def stream_core(inputs_f, step_size, b_rows, c_rows, decay_rate, skip_gain):
    blocks = (inputs_f.reshape(-1, TOK_DEV, INNER), step_size.reshape(-1, TOK_DEV, HEADS), b_rows.reshape(-1, TOK_DEV, STATE), c_rows.reshape(-1, TOK_DEV, STATE))
    start_state = jnp.zeros((STATE, INNER), jnp.float32)
    final_state, outputs = lax.scan(partial(block_pass, decay_rate, skip_gain), start_state, blocks)
    return outputs.reshape(SEQ_LEN, INNER)

def reference(features, head_inputs, out_grad, bc_weight, dt_weight, dt_bias, decay_rate, skip_gain):
    joined = jnp.concatenate([bc_weight, dt_weight], axis=1)

    def one_stream(total, stream):
        feature_rows, input_rows, grad_rows = stream
        projection = jnp.dot(feature_rows, joined, preferred_element_type=jnp.float32)
        b_rows = projection[:, :STATE]
        c_rows = projection[:, STATE:2 * STATE]
        pre_step = projection[:, 2 * STATE:] + dt_bias[None, :]
        step_size = jax.nn.softplus(pre_step)
        inputs_f = input_rows.astype(jnp.float32)

        def core_fn(first, second, third, fourth):
            return stream_core(first, second, third, fourth, decay_rate, skip_gain)
        output, pullback = jax.vjp(core_fn, inputs_f, step_size, b_rows, c_rows)
        inputs_grad, step_grad, b_grad, c_grad = pullback(grad_rows.astype(jnp.float32))
        pre_grad = step_grad * jax.nn.sigmoid(pre_step)
        proj_grad = jnp.concatenate([b_grad, c_grad, pre_grad], axis=1).astype(jnp.bfloat16)
        feature_grad = lax.dot_general(proj_grad, joined, (((1,), (1,)), ((), ())), preferred_element_type=jnp.float32).astype(jnp.bfloat16)
        total = total + lax.dot_general(feature_rows, proj_grad, (((0,), (0,)), ((), ())), preferred_element_type=jnp.float32)
        return (total, (feature_grad, inputs_grad.astype(jnp.bfloat16)))
    start_total = jnp.zeros((D, 2 * STATE + HEADS), jnp.float32)
    total, results = lax.scan(one_stream, start_total, (features, head_inputs, out_grad))
    input_grad, head_grad = results
    total = total * (1.0 / math.sqrt(STREAMS * SEQ_LEN))
    return (input_grad, head_grad, total[:, :2 * STATE], total[:, 2 * STATE:])
```

```python
import math

import jax
import jax.numpy as jnp
from jax import lax
from jax.experimental import pallas as pl
from jax.experimental.pallas import tpu as pltpu
from jax.sharding import PartitionSpec as P

bf16, f32 = jnp.bfloat16, jnp.float32
highest = lax.Precision.HIGHEST

HEADS = 40
PAIRS = 20
TOK = 128
WIDE = 2560
ROWS = 80
DP = 32
SEQ = 16
HALF = 64
LANES = 128

NN = (((1,), (0,)), ((), ()))
NT = (((1,), (1,)), ((), ()))
TN = (((0,), (0,)), ((), ()))


def iota(shape, axis):
    return lax.broadcasted_iota(jnp.int32, shape, axis)


def ones_where(mask, dtype=f32):
    return jnp.where(mask, 1.0, 0.0).astype(dtype)


def mm(a, b, dims=NN):
    return lax.dot_general(a.astype(bf16), b.astype(bf16), dims, preferred_element_type=f32)


def high_low(value):
    high = value.astype(bf16)
    return high, (value - high.astype(f32)).astype(bf16)


def mm_exact(a, b, dims=NN):
    return lax.dot_general(a, b, dims, precision=highest, preferred_element_type=f32)


def head_of_lane(lane):
    return lane - jnp.where(lane >= 40, 40, 0) - jnp.where(lane >= 80, 40, 0)


def interleave(shape, source_axis):
    source, target = iota(shape, source_axis), iota(shape, 1 - source_axis)
    low = target & 7
    wanted = 4 * (target >> 3) + low + jnp.where(low >= 4, 60, 0)
    return ones_where(source == wanted)


def triple(row):
    place = ones_where(iota((HEADS, LANES), 0) == head_of_lane(iota((HEADS, LANES), 1)))
    return mm_exact(jnp.broadcast_to(row, (8, HEADS)), place)[0:1]


def split(value):
    lane = iota(value.shape, 1)
    first = value.astype(bf16).astype(f32)
    rest = value - first
    second = rest.astype(bf16).astype(f32)
    third = rest - second
    return jnp.where(lane < 40, first, jnp.where(lane < 80, second, third)).astype(bf16)


def spread_matrix(pair):
    k, lane = iota((LANES, LANES), 0), iota((LANES, LANES), 1)
    return ones_where(head_of_lane(k) == 2 * pair + (lane >> 6), bf16)


def gather_matrix(pair):
    lane, k = iota((LANES, LANES), 0), iota((LANES, LANES), 1)
    return ones_where(head_of_lane(k) == 2 * pair + (lane >> 6), bf16)


def pack_kernel(core_ref, bc_ref, dt_ref, out_ref):
    bc = mm(bc_ref[...], interleave((LANES, LANES), 0))
    row, lane = iota((HEADS, LANES), 0), iota((HEADS, LANES), 1)
    dt = dt_ref[...]
    packed = mm(dt[0:32], ones_where(lane == row)) + mm(dt[32:64], ones_where(lane == row + 40))
    last = mm(dt[64:80], ones_where(lane == row + 80))
    zeros = jnp.zeros((16, LANES), f32)
    packed = packed + jnp.concatenate([last, zeros], axis=0)
    second = jnp.concatenate([bc[64:80], packed, zeros], axis=0)
    value = jnp.where(core_ref[0] == 0, bc[0:64], second).astype(bf16)
    for owner in range(DP):
        out_ref[owner] = value


def first_kernel(
    core_ref, mine_ref, other_ref, feat_ref, x_ref, g_ref, bias_ref, rate_ref,
    weight_ref, proj_ref, pre_ref, cum_ref, state_ref,
):
    lane16 = iota((16, LANES), 1)
    group = [
        ones_where((lane16 >= 40 * k) & (lane16 < 40 * k + 40), bf16) for k in range(3)
    ]

    def assemble(one_ref, two_ref):
        for owner in range(DP):
            base = ROWS * owner
            weight_ref[base : base + 64, 0:LANES] = one_ref[owner]
            weight_ref[base + 64 : base + 80, 0:LANES] = two_ref[owner, 0:16, :]
            low, high = two_ref[owner, 16:32, :], two_ref[owner, 32:48, :]
            weight_ref[base : base + 16, LANES:] = low * group[0]
            weight_ref[base + 16 : base + 32, LANES:] = high * group[0]
            weight_ref[base + 32 : base + 48, LANES:] = low * group[1]
            weight_ref[base + 48 : base + 64, LANES:] = high * group[1]
            weight_ref[base + 64 : base + 80, LANES:] = low * group[2]

    core = core_ref[0]

    @pl.when(core == 0)
    def _():
        assemble(mine_ref, other_ref)

    @pl.when(core != 0)
    def _():
        assemble(other_ref, mine_ref)

    both = lax.dot_general(feat_ref[...], weight_ref[...], NN, preferred_element_type=f32)
    proj = both[:, 0:LANES]
    row, lane = iota((LANES, LANES), 0), iota((LANES, LANES), 1)
    head_row, head_lane = head_of_lane(row), head_of_lane(lane)
    fold = ones_where((head_row == head_lane) & (head_lane < HEADS))
    pre = mm_exact(both[:, LANES:], fold) + triple(bias_ref[...])
    step = jnp.maximum(pre, 0.0) + jnp.log1p(jnp.exp(-jnp.abs(pre)))
    cum = mm_exact(ones_where(row >= lane), -triple(rate_ref[...]) * step)
    proj_ref[...] = proj
    pre_ref[...] = pre
    cum_ref[...] = cum
    total = cum[TOK - 1 : TOK]
    stacked = jnp.concatenate(
        [split(step * jnp.exp(total - cum)), split(jnp.exp(cum))], axis=0
    )
    turned_high, turned_low = high_low(proj.T)
    both_turned = jnp.concatenate([turned_high, turned_low], axis=0)
    forward = (row & 7) < 4

    def block(pair):
        cols = slice(LANES * pair, LANES * pair + LANES)
        wide = lax.dot_general(stacked, spread_matrix(pair), NN, preferred_element_type=f32)
        ending = x_ref[:, cols].astype(f32) * wide[0:TOK]
        weighted = g_ref[:, cols].astype(f32) * wide[TOK:]
        high, low = high_low(jnp.concatenate([ending, weighted], axis=1))
        joined = mm(both_turned, high)
        joined = joined[0:LANES] + (joined[LANES:] + mm(turned_high, low))
        return jnp.where(forward, joined[:, 0:LANES], joined[:, LANES:]).reshape(SEQ, 8, LANES)

    for two in range(PAIRS // 2):
        value = jnp.concatenate([block(2 * two), block(2 * two + 1)], axis=1)
        state_ref[:, 16 * two : 16 * two + 16, :] = value.astype(bf16)
    decay = split(jnp.broadcast_to(total, (16, LANES)))
    for owner in range(SEQ):
        state_ref[owner, 160:176, :] = decay


def chain_kernel(state_ref, out_ref):
    row16 = iota((16, LANES), 0)
    logs = jnp.zeros((16, LANES), f32)
    for place in range(SEQ):
        logs = logs + jnp.where(row16 == place, state_ref[place, 160:176, :].astype(f32), 0.0)
    logs = logs.astype(bf16)
    forward = (row16 & 7) < 4
    for two in range(PAIRS // 2):
        rows = slice(16 * two, 16 * two + 16)
        factor = [
            jnp.exp(
                lax.dot_general(
                    logs, spread_matrix(2 * two + k), NN, preferred_element_type=f32
                )
            )
            for k in range(2)
        ]

        def decay(place):
            return jnp.concatenate(
                [jnp.broadcast_to(factor[k][place : place + 1], (8, LANES)) for k in range(2)],
                axis=0,
            )

        values = [state_ref[place, rows, :].astype(f32) for place in range(SEQ)]
        decays = [decay(place) for place in range(SEQ)]
        ahead = [jnp.zeros((16, LANES), f32)]
        for place in range(SEQ - 1):
            ahead.append(ahead[-1] * decays[place] + values[place])
        back = jnp.zeros((16, LANES), f32)
        for place in range(SEQ - 1, -1, -1):
            out_ref[place, rows, :] = jnp.where(forward, ahead[place], back).astype(bf16)
            back = back * decays[place] + values[place]


def softplus(pre):
    return jnp.maximum(pre, 0.0) + jnp.log1p(jnp.exp(-jnp.abs(pre)))


def inside_kernel(
    proj_ref, pre_ref, cum_ref, x_ref, g_ref, scaled_ref, across_ref, later_ref, own_ref, rows_ref
):
    proj, cum = proj_ref[...], cum_ref[...]
    step = softplus(pre_ref[...])
    row, lane = iota((LANES, LANES), 0), iota((LANES, LANES), 1)
    low = (lane & 7) < 4
    b_low = jnp.where(low, proj, 0.0)
    c_low = jnp.where(low, pltpu.roll(proj, LANES - 4, 1), 0.0)
    meet = mm_exact(b_low, c_low, NT)
    causal = lane >= row
    cum_turned = cum.T
    lane_head = head_of_lane(lane)
    across = jnp.zeros((TOK, TOK), f32)
    own = jnp.zeros((TOK, LANES), f32)
    first_half = ones_where(lane < 64, bf16)
    second_half = ones_where(lane >= 64, bf16)
    rows_ref[...] = jnp.zeros_like(rows_ref)
    for pair in range(PAIRS):
        cols = slice(LANES * pair, LANES * pair + LANES)
        x, g = x_ref[:, cols], g_ref[:, cols]
        mixed, parts = [], []
        for which, half in enumerate((first_half, second_half)):
            head = 2 * pair + which
            g_half = g * half
            outer = lax.dot_general(x, g_half, NT, preferred_element_type=f32)
            gap = cum_turned[head : head + 1, :] - cum[:, head : head + 1]
            weight = jnp.exp(jnp.where(causal, gap, -1e30))
            step_col = step[:, head : head + 1]
            spot = outer * weight
            across = across + spot * step_col
            product = spot * meet
            own = jnp.where(lane_head == head, jnp.sum(product, axis=1, keepdims=True), own)
            rows_ref[head : head + 1, :] = jnp.sum(product * step_col, axis=0, keepdims=True)
            mixed.append((meet * weight).astype(bf16))
            parts.append(g_half)
        scaled_ref[:, cols] = lax.dot_general(
            jnp.concatenate(mixed, axis=1), jnp.concatenate(parts, axis=0), NN,
            preferred_element_type=f32,
        )
    across_ref[...] = across
    own_ref[...] = own
    place = ones_where((row == lane_head) & (row < HEADS))
    later_ref[...] = mm_exact(rows_ref[...].T, place)


def last_kernel(
    core_ref, carried_ref, weight_ref, proj_ref, pre_ref, cum_ref, scaled_ref, across_ref,
    later_ref, own_ref, feat_ref, x_ref, g_ref, rate_ref, skip_ref,
    input_grad_ref, head_grad_ref, keep_ref, send_ref,
):
    proj, pre, cum = proj_ref[...], pre_ref[...], cum_ref[...]
    step = softplus(pre)
    total = cum[TOK - 1 : TOK]
    row, lane = iota((LANES, LANES), 0), iota((LANES, LANES), 1)
    low = (lane & 7) < 4
    c_low = jnp.where(low, pltpu.roll(proj, LANES - 4, 1), 0.0)
    b_high = jnp.where(low, 0.0, pltpu.roll(proj, 4, 1))
    left = jnp.concatenate([c_low, b_high], axis=0)
    left = jnp.concatenate(high_low(left), axis=0)
    stacked = jnp.concatenate(
        [
            split(step),
            split(jnp.exp(total - cum)),
            split(jnp.exp(cum)),
            split(jnp.broadcast_to(triple(skip_ref[...]), (16, LANES))),
        ],
        axis=0,
    )
    crossed = jnp.zeros((4 * TOK, LANES), f32)
    sums = jnp.zeros((4 * TOK + 32, LANES), f32)
    low_rows = (row & 7) < 4
    for two in range(PAIRS // 2):
        chunk = carried_ref[:, 16 * two : 16 * two + 16, :].astype(f32)
        for which in range(2):
            pair = 2 * two + which
            cols = slice(LANES * pair, LANES * pair + LANES)
            state = chunk[:, 8 * which : 8 * which + 8, :].reshape(LANES, LANES)
            state_b = state.astype(bf16)
            wide = lax.dot_general(stacked, spread_matrix(pair), NN, preferred_element_type=f32)
            step_w, end_w, start_w = wide[0:TOK], wide[TOK : 2 * TOK], wide[2 * TOK : 3 * TOK]
            skip_w = wide[3 * TOK : 3 * TOK + 1]
            x, g = x_ref[:, cols].astype(f32), g_ref[:, cols].astype(f32)
            weighted = g * start_w
            ending = x * end_w
            pushed = lax.dot_general(left, state_b, NN, preferred_element_type=f32)
            pushed = pushed[0 : 2 * TOK] + pushed[2 * TOK :]
            out, reach = pushed[0:TOK], pushed[TOK:]
            lines = jnp.concatenate([weighted, ending * step_w], axis=0)
            crossed = crossed + mm(jnp.concatenate(high_low(lines), axis=0), state_b, NT)
            pairing = jnp.where(low_rows, state * pltpu.roll(state, LANES - 4, 0), 0.0)
            pairing = jnp.sum(pairing.reshape(SEQ, 8, LANES), axis=0)
            pairing = jnp.concatenate([pairing, jnp.zeros((8, LANES), f32)], axis=0)
            lines = jnp.concatenate([weighted * out, ending * reach, pairing], axis=0)
            sums = sums + mm(jnp.concatenate(high_low(lines), axis=0), gather_matrix(pair))
            whole = scaled_ref[:, cols] + end_w * reach
            head_grad_ref[:, cols] = (g * skip_w + step_w * whole).astype(bf16)
    crossed = crossed[0 : 2 * TOK] + crossed[2 * TOK :]
    sums = sums[0 : 2 * TOK + 16] + sums[2 * TOK + 16 :]
    through, reached = sums[0:TOK], sums[TOK : 2 * TOK]
    paired = jnp.sum(sums[2 * TOK : 2 * TOK + 8], axis=0, keepdims=True)
    own = own_ref[...]
    decay_grad = (
        mm_exact(ones_where(lane >= row), later_ref[...] - step * own + through)
        + mm_exact(ones_where(lane < row), step * reached)
        + jnp.exp(total) * paired
    )
    step_grad = own + reached - triple(rate_ref[...]) * decay_grad
    pre_grad = step_grad * jax.nn.sigmoid(pre)
    pre_grad = jnp.where(lane < 3 * HEADS, pre_grad, 0.0)
    across = across_ref[...]
    bc_grad = mm_exact(across, c_low) + mm_exact(across.T, b_high)
    bc_grad = bc_grad + jnp.where(
        low, pltpu.roll(crossed[TOK:], LANES - 4, 1), pltpu.roll(crossed[0:TOK], 4, 1)
    )
    grads = high_low(jnp.concatenate([bc_grad, pre_grad], axis=1))
    tall, flat = jnp.concatenate(grads, axis=0), jnp.concatenate(grads, axis=1)
    for part in range(10):
        cols = slice(256 * part, 256 * part + 256)
        product = lax.dot_general(tall, weight_ref[cols, :], NT, preferred_element_type=f32)
        input_grad_ref[:, cols] = (product[0:TOK] + product[TOK:]).astype(bf16)
    first_core = core_ref[0] == 0
    lane32 = iota((32, LANES), 1)
    zeros = jnp.zeros((16, LANES), f32)
    for part in range(4):
        cols = slice(640 * part, 640 * part + 640)
        product = lax.dot_general(feat_ref[:, cols], flat, TN, preferred_element_type=f32)
        product = product[:, 0 : 2 * LANES] + product[:, 2 * LANES :]
        for inner in range(8):
            base = ROWS * inner
            dt = product[base : base + 80, LANES:]
            packed = jnp.where(
                lane32 < 40,
                dt[0:32],
                jnp.where(lane32 < 80, dt[32:64], jnp.concatenate([dt[64:80], zeros], axis=0)),
            )
            one = product[base : base + 64, 0:LANES]
            two = jnp.concatenate([product[base + 64 : base + 80, 0:LANES], packed, zeros], axis=0)
            owner = 8 * part + inner
            keep_ref[owner] = jnp.where(first_core, one, two)
            send_ref[owner] = jnp.where(first_core, two, one).astype(bf16)


def finish_kernel(parts_ref, bc_ref, dt_ref):
    one = parts_ref[0].astype(f32)
    two = parts_ref[1].astype(f32)
    for place in range(2, SEQ, 2):
        one = one + parts_ref[place].astype(f32)
        two = two + parts_ref[place + 1].astype(f32)
    scale = 1.0 / math.sqrt(SEQ * DP * TOK)
    bc = jnp.concatenate([one, two[0:16]], axis=0) * scale
    bc_ref[...] = mm_exact(bc, interleave((LANES, LANES), 1))
    packed = two[16:48] * scale
    lane, column = iota((LANES, HEADS), 0), iota((LANES, HEADS), 1)
    for k in range(3):
        rows = min(32, ROWS - 32 * k)
        dt_ref[32 * k : 32 * k + rows, :] = mm_exact(
            packed[0:rows], ones_where(lane == column + 40 * k)
        )


def call(kernel, name, out_shape, scalars, arrays, scratch=(), flops=0, bytes_accessed=0):
    smem = pl.BlockSpec(memory_space=pltpu.SMEM)
    vmem = pl.BlockSpec(memory_space=pltpu.VMEM)
    return pl.pallas_call(
        kernel,
        name=name,
        out_shape=out_shape,
        in_specs=[smem] * len(scalars) + [vmem] * len(arrays),
        out_specs=jax.tree.map(lambda _: vmem, out_shape),
        scratch_shapes=scratch,
        compiler_params=pltpu.CompilerParams(vmem_limit_bytes=40 << 20),
        cost_estimate=pl.CostEstimate(
            flops=flops, bytes_accessed=bytes_accessed, transcendentals=0
        ),
    )(*scalars, *arrays)


def shape(dims, dtype):
    return jax.ShapeDtypeStruct(dims, dtype)


SWAP = [(place, place ^ 1) for place in range(SEQ)]


def body(features, head_inputs, out_grad, bc_weight, dt_weight, dt_bias, decay_rate, skip_gain):
    core = (lax.axis_index("seq") & 1).astype(jnp.int32).reshape(1)
    feats, x, g = features[0], head_inputs[0], out_grad[0]
    bias, rate, skip = dt_bias[None], decay_rate[None], skip_gain[None]
    square = shape((TOK, LANES), f32)
    chunks = shape((DP, HALF, LANES), bf16)

    sent = call(pack_kernel, "pack", chunks, [core], [bc_weight, dt_weight])
    mine = lax.all_to_all(sent, "dp", 0, 0, tiled=True)
    other = lax.ppermute(mine, "seq", SWAP)
    weight, proj, pre, cum, local = call(
        first_kernel,
        "first",
        (shape((WIDE, 2 * LANES), bf16), square, square, square, shape((SEQ, 176, LANES), bf16)),
        [core],
        [mine, other, feats, x, g, bias, rate],
    )
    gathered = lax.all_to_all(local, "seq", 0, 0, tiled=True)
    scaled, across, later, own = call(
        inside_kernel,
        "inside",
        (shape((TOK, WIDE), f32), square, square, square),
        [],
        [proj, pre, cum, x, g],
        scratch=[pltpu.VMEM((LANES, TOK), f32)],
        flops=400_000_000,
        bytes_accessed=4_000_000,
    )
    entering = call(chain_kernel, "chain", shape((SEQ, 160, LANES), bf16), [], [gathered])
    carried = lax.all_to_all(entering, "seq", 0, 0, tiled=True)
    input_grad, head_grad, keep, send = call(
        last_kernel,
        "last",
        (shape((TOK, WIDE), bf16), shape((TOK, WIDE), bf16), shape((DP, HALF, LANES), f32), chunks),
        [core],
        [carried, weight, proj, pre, cum, scaled, across, later, own, feats, x, g, rate, skip],
    )
    paired = (keep + lax.ppermute(send, "seq", SWAP).astype(f32)).astype(bf16)
    owned = lax.all_to_all(paired, "dp", 0, 0, tiled=True)
    owned = jnp.sum(owned.astype(f32), axis=0)
    parts = lax.all_gather(owned, "seq")
    bc_grad, dt_grad = call(
        finish_kernel, "finish", (shape((ROWS, LANES), f32), shape((ROWS, HEADS), f32)), [], [parts]
    )
    return input_grad[None], head_grad[None], bc_grad, dt_grad


def solution(mesh):
    in_specs = (
        P("dp", "seq", None),
        P("dp", "seq", None),
        P("dp", "seq", None),
        P("dp", None),
        P("dp", None),
        P(),
        P(),
        P(),
    )
    out_specs = (P("dp", "seq", None), P("dp", "seq", None), P("dp", None), P("dp", None))
    return jax.shard_map(body, mesh=mesh, in_specs=in_specs, out_specs=out_specs, check_vma=False)
```

```python
import math
from functools import partial

import jax
import jax.numpy as jnp
from jax import lax
from jax.experimental import pallas as pl
from jax.experimental.pallas import tpu as pltpu
from jax.sharding import PartitionSpec as P

bf16, f32 = jnp.bfloat16, jnp.float32
highest = lax.Precision.HIGHEST

HEADS = 40
PAIRS = 20
TOK = 128
WIDE = 2560
ROWS = 80
DP = 32
SEQ = 16
HALF = 56
REST = 24
LANES = 128

NN = (((1,), (0,)), ((), ()))
NT = (((1,), (1,)), ((), ()))
TN = (((0,), (0,)), ((), ()))


def iota(shape, axis):
    return lax.broadcasted_iota(jnp.int32, shape, axis)


def ones_where(mask, dtype=f32):
    return jnp.where(mask, 1.0, 0.0).astype(dtype)


def mm(a, b, dims=NN):
    return lax.dot_general(a.astype(bf16), b.astype(bf16), dims, preferred_element_type=f32)


def high_low(value):
    high = value.astype(bf16)
    return high, (value - high.astype(f32)).astype(bf16)


def mm_exact(a, b, dims=NN):
    return lax.dot_general(a, b, dims, precision=highest, preferred_element_type=f32)


def head_of_lane(lane):
    return lane - jnp.where(lane >= 40, 40, 0) - jnp.where(lane >= 80, 40, 0)


def interleave(shape, source_axis):
    source, target = iota(shape, source_axis), iota(shape, 1 - source_axis)
    low = target & 7
    wanted = 4 * (target >> 3) + low + jnp.where(low >= 4, 60, 0)
    return ones_where(source == wanted)


def triple(row):
    place = ones_where(iota((HEADS, LANES), 0) == head_of_lane(iota((HEADS, LANES), 1)))
    return mm_exact(jnp.broadcast_to(row, (8, HEADS)), place)[0:1]


def split(value):
    lane = iota(value.shape, 1)
    first = value.astype(bf16).astype(f32)
    rest = value - first
    second = rest.astype(bf16).astype(f32)
    third = rest - second
    return jnp.where(lane < 40, first, jnp.where(lane < 80, second, third)).astype(bf16)


def spread_matrix(pair):
    k, lane = iota((LANES, LANES), 0), iota((LANES, LANES), 1)
    return ones_where(head_of_lane(k) == 2 * pair + (lane >> 6), bf16)


def gather_matrix(pair):
    lane, k = iota((LANES, LANES), 0), iota((LANES, LANES), 1)
    return ones_where(head_of_lane(k) == 2 * pair + (lane >> 6), bf16)


def pack_kernel(core_ref, bc_ref, dt_ref, out_ref):
    bc = mm(bc_ref[...], interleave((LANES, LANES), 0))
    row, lane = iota((HEADS, LANES), 0), iota((HEADS, LANES), 1)
    dt = [mm(dt_ref[...], ones_where(lane == row + 40 * k), TN) for k in range(3)]
    last = jnp.concatenate([dt[2][64:80], jnp.zeros((16, LANES), f32)], axis=0)
    packed = dt[0][0:32] + dt[1][32:64] + last
    second = jnp.concatenate([bc[HALF:ROWS], packed], axis=0)
    value = jnp.where(core_ref[0] == 0, bc[0:HALF], second).astype(bf16)
    for owner in range(DP):
        out_ref[owner] = value


def turn_kernel(feat_ref, out_ref):
    for part in range(PAIRS):
        rows = slice(LANES * part, LANES * part + LANES)
        out_ref[rows, :] = feat_ref[:, rows].T


def first_kernel(
    core_ref, mine_ref, other_ref, feat_ref, x_ref, g_ref, bias_ref, rate_ref,
    weight_ref, proj_ref, pre_ref, cum_ref, state_ref,
):
    lane16 = iota((16, LANES), 1)
    group = [
        ones_where((lane16 >= 40 * k) & (lane16 < 40 * k + 40), bf16) for k in range(3)
    ]

    def assemble(one_ref, two_ref):
        for owner in range(DP):
            base = ROWS * owner
            weight_ref[base : base + HALF, 0:LANES] = one_ref[owner]
            weight_ref[base + HALF : base + ROWS, 0:LANES] = two_ref[owner, 0:REST, :]
            low, high = two_ref[owner, 24:40, :], two_ref[owner, 40:56, :]
            weight_ref[base : base + 16, LANES:] = low * group[0]
            weight_ref[base + 16 : base + 32, LANES:] = high * group[0]
            weight_ref[base + 32 : base + 48, LANES:] = low * group[1]
            weight_ref[base + 48 : base + 64, LANES:] = high * group[1]
            weight_ref[base + 64 : base + 80, LANES:] = low * group[2]

    core = core_ref[0]

    @pl.when(core == 0)
    def _():
        assemble(mine_ref, other_ref)

    @pl.when(core != 0)
    def _():
        assemble(other_ref, mine_ref)

    both = lax.dot_general(feat_ref[...], weight_ref[...], NN, preferred_element_type=f32)
    proj = both[:, 0:LANES]
    row, lane = iota((LANES, LANES), 0), iota((LANES, LANES), 1)
    head_row, head_lane = head_of_lane(row), head_of_lane(lane)
    fold = ones_where((head_row == head_lane) & (head_lane < HEADS))
    pre = mm_exact(both[:, LANES:], fold) + triple(bias_ref[...])
    step = jnp.maximum(pre, 0.0) + jnp.log1p(jnp.exp(-jnp.abs(pre)))
    cum = mm_exact(ones_where(row >= lane), -triple(rate_ref[...]) * step)
    proj_ref[...] = proj
    pre_ref[...] = pre
    cum_ref[...] = cum
    total = cum[TOK - 1 : TOK]
    stacked = jnp.concatenate(
        [split(step * jnp.exp(total - cum)), split(jnp.exp(cum))], axis=0
    )
    turned_high, turned_low = high_low(proj.T)
    both_turned = jnp.concatenate([turned_high, turned_low], axis=0)
    forward = (row & 7) < 4

    def block(pair):
        cols = slice(LANES * pair, LANES * pair + LANES)
        wide = lax.dot_general(stacked, spread_matrix(pair), NN, preferred_element_type=f32)
        ending = x_ref[:, cols].astype(f32) * wide[0:TOK]
        weighted = g_ref[:, cols].astype(f32) * wide[TOK:]
        high, low = high_low(jnp.concatenate([ending, weighted], axis=1))
        joined = mm(both_turned, high)
        joined = joined[0:LANES] + (joined[LANES:] + mm(turned_high, low))
        return jnp.where(forward, joined[:, 0:LANES], joined[:, LANES:]).reshape(SEQ, 8, LANES)

    for two in range(PAIRS // 2):
        value = jnp.concatenate([block(2 * two), block(2 * two + 1)], axis=1)
        state_ref[:, 16 * two : 16 * two + 16, :] = value.astype(bf16)
    decay = split(jnp.broadcast_to(total, (8, LANES)))
    for owner in range(SEQ):
        state_ref[owner, 160:168, :] = decay


def chain_kernel(state_ref, after_ref, out_ref):
    row16 = iota((16, LANES), 0)
    logs = jnp.zeros((16, LANES), f32)
    for place in range(SEQ):
        line = state_ref[place, 160:168, :].astype(f32)
        logs = logs + jnp.where(row16 == place, jnp.concatenate([line, line], axis=0), 0.0)
    logs = logs.astype(bf16)
    forward = (row16 & 7) < 4
    for two in range(PAIRS // 2):
        rows = slice(16 * two, 16 * two + 16)
        factor = [
            jnp.exp(
                lax.dot_general(
                    logs, spread_matrix(2 * two + k), NN, preferred_element_type=f32
                )
            )
            for k in range(2)
        ]

        def decay(place):
            return jnp.concatenate(
                [jnp.broadcast_to(factor[k][place : place + 1], (8, LANES)) for k in range(2)],
                axis=0,
            )

        values = [state_ref[place, rows, :].astype(f32) for place in range(SEQ)]
        decays = [decay(place) for place in range(SEQ)]
        ahead = [jnp.zeros((16, LANES), f32)]
        for place in range(SEQ - 1):
            ahead.append(ahead[-1] * decays[place] + values[place])
        back = jnp.zeros((16, LANES), f32)
        for place in range(SEQ - 1, -1, -1):
            out_ref[place, rows, :] = jnp.where(forward, ahead[place], back).astype(bf16)
            back = back * decays[place] + values[place]


def softplus(pre):
    return jnp.maximum(pre, 0.0) + jnp.log1p(jnp.exp(-jnp.abs(pre)))


def inside_kernel(first_pair, start, *refs):
    proj_ref, pre_ref, cum_ref, x_ref, g_ref = refs[:5]
    scaled_ref, across_ref, own_ref, rows_ref = refs[-4:]
    proj, cum = proj_ref[...], cum_ref[...]
    step = softplus(pre_ref[...])
    row, lane = iota((LANES, LANES), 0), iota((LANES, LANES), 1)
    low = (lane & 7) < 4
    b_low = jnp.where(low, proj, 0.0)
    c_low = jnp.where(low, pltpu.roll(proj, LANES - 4, 1), 0.0)
    meet = mm_exact(b_low, c_low, NT)
    causal = lane >= row
    cum_turned = cum.T
    lane_head = head_of_lane(lane)
    if start:
        across = jnp.zeros((TOK, TOK), f32)
        own = jnp.zeros((TOK, LANES), f32)
        rows_ref[...] = jnp.zeros_like(rows_ref)
    else:
        across, own = refs[5][...], refs[6][...]
        rows_ref[...] = refs[7][...]
    first_half = ones_where(lane < 64, bf16)
    second_half = ones_where(lane >= 64, bf16)
    for pair in range(first_pair, first_pair + PAIRS // 2):
        cols = slice(LANES * pair, LANES * pair + LANES)
        x, g = x_ref[:, cols], g_ref[:, cols]
        mixed, parts = [], []
        for which, half in enumerate((first_half, second_half)):
            head = 2 * pair + which
            g_half = g * half
            outer = lax.dot_general(x, g_half, NT, preferred_element_type=f32)
            gap = cum_turned[head : head + 1, :] - cum[:, head : head + 1]
            weight = jnp.exp(jnp.where(causal, gap, -1e30))
            step_col = step[:, head : head + 1]
            spot = outer * weight
            across = across + spot * step_col
            product = spot * meet
            own = jnp.where(lane_head == head, jnp.sum(product, axis=1, keepdims=True), own)
            rows_ref[head : head + 1, :] = jnp.sum(product * step_col, axis=0, keepdims=True)
            mixed.append((meet * weight).astype(bf16))
            parts.append(g_half)
        here = slice(LANES * (pair - first_pair), LANES * (pair - first_pair) + LANES)
        scaled_ref[:, here] = lax.dot_general(
            jnp.concatenate(mixed, axis=1), jnp.concatenate(parts, axis=0), NN,
            preferred_element_type=f32,
        )
    across_ref[...] = across
    own_ref[...] = own


def last_kernel(
    core_ref, carried_ref, proj_ref, pre_ref, cum_ref, left_ref, right_ref, across_ref,
    own_ref, rows_ref, turned_ref, x_ref, g_ref, rate_ref, skip_ref,
    grads_ref, head_grad_ref, keep_ref, send_ref,
):
    proj, pre, cum = proj_ref[...], pre_ref[...], cum_ref[...]
    step = softplus(pre)
    total = cum[TOK - 1 : TOK]
    row, lane = iota((LANES, LANES), 0), iota((LANES, LANES), 1)
    low = (lane & 7) < 4
    c_low = jnp.where(low, pltpu.roll(proj, LANES - 4, 1), 0.0)
    b_high = jnp.where(low, 0.0, pltpu.roll(proj, 4, 1))
    left = jnp.concatenate([c_low, b_high], axis=0)
    left = jnp.concatenate(high_low(left), axis=0)
    stacked = jnp.concatenate(
        [
            split(step),
            split(jnp.exp(total - cum)),
            split(jnp.exp(cum)),
            split(jnp.broadcast_to(triple(skip_ref[...]), (16, LANES))),
        ],
        axis=0,
    )
    crossed = jnp.zeros((4 * TOK, LANES), f32)
    sums = jnp.zeros((4 * TOK + 32, LANES), f32)
    low_rows = (row & 7) < 4
    for two in range(PAIRS // 2):
        chunk = carried_ref[:, 16 * two : 16 * two + 16, :].astype(f32)
        for which in range(2):
            pair = 2 * two + which
            cols = slice(LANES * pair, LANES * pair + LANES)
            state = chunk[:, 8 * which : 8 * which + 8, :].reshape(LANES, LANES)
            state_b = state.astype(bf16)
            wide = lax.dot_general(stacked, spread_matrix(pair), NN, preferred_element_type=f32)
            step_w, end_w, start_w = wide[0:TOK], wide[TOK : 2 * TOK], wide[2 * TOK : 3 * TOK]
            skip_w = wide[3 * TOK : 3 * TOK + 1]
            x, g = x_ref[:, cols].astype(f32), g_ref[:, cols].astype(f32)
            weighted = g * start_w
            ending = x * end_w
            pushed = lax.dot_general(left, state_b, NN, preferred_element_type=f32)
            pushed = pushed[0 : 2 * TOK] + pushed[2 * TOK :]
            out, reach = pushed[0:TOK], pushed[TOK:]
            lines = jnp.concatenate([weighted, ending * step_w], axis=0)
            crossed = crossed + mm(jnp.concatenate(high_low(lines), axis=0), state_b, NT)
            pairing = jnp.where(low_rows, state * pltpu.roll(state, LANES - 4, 0), 0.0)
            pairing = jnp.sum(pairing.reshape(SEQ, 8, LANES), axis=0)
            pairing = jnp.concatenate([pairing, jnp.zeros((8, LANES), f32)], axis=0)
            lines = jnp.concatenate([weighted * out, ending * reach, pairing], axis=0)
            sums = sums + mm(jnp.concatenate(high_low(lines), axis=0), gather_matrix(pair))
            half_ref = left_ref if two < 5 else right_ref
            first_lane = LANES * (pair % 10)
            whole = half_ref[:, first_lane : first_lane + LANES] + end_w * reach
            head_grad_ref[:, cols] = (g * skip_w + step_w * whole).astype(bf16)
    crossed = crossed[0 : 2 * TOK] + crossed[2 * TOK :]
    sums = sums[0 : 2 * TOK + 16] + sums[2 * TOK + 16 :]
    through, reached = sums[0:TOK], sums[TOK : 2 * TOK]
    paired = jnp.sum(sums[2 * TOK : 2 * TOK + 8], axis=0, keepdims=True)
    own = own_ref[...]
    lane_head = head_of_lane(lane)
    later = mm_exact(rows_ref[...].T, ones_where((row == lane_head) & (row < HEADS)))
    decay_grad = (
        mm_exact(ones_where(lane >= row), later - step * own + through)
        + mm_exact(ones_where(lane < row), step * reached)
        + jnp.exp(total) * paired
    )
    step_grad = own + reached - triple(rate_ref[...]) * decay_grad
    pre_grad = step_grad * jax.nn.sigmoid(pre)
    pre_grad = jnp.where(lane < 3 * HEADS, pre_grad, 0.0)
    across = across_ref[...]
    bc_grad = mm_exact(across, c_low) + mm_exact(across.T, b_high)
    bc_grad = bc_grad + jnp.where(
        low, pltpu.roll(crossed[TOK:], LANES - 4, 1), pltpu.roll(crossed[0:TOK], 4, 1)
    )
    grads = high_low(jnp.concatenate([bc_grad, pre_grad], axis=1))
    tall, flat = jnp.concatenate(grads, axis=0), jnp.concatenate(grads, axis=1)
    grads_ref[...] = tall
    first_core = core_ref[0] == 0
    lane32 = iota((32, LANES), 1)
    zeros = jnp.zeros((16, LANES), f32)
    for part in range(4):
        rows = slice(640 * part, 640 * part + 640)
        product = lax.dot_general(turned_ref[rows, :], flat, NN, preferred_element_type=f32)
        product = product[:, 0 : 2 * LANES] + product[:, 2 * LANES :]
        for inner in range(8):
            base = ROWS * inner
            dt = product[base : base + ROWS, LANES:]
            packed = jnp.where(
                lane32 < 40,
                dt[0:32],
                jnp.where(lane32 < 80, dt[32:64], jnp.concatenate([dt[64:80], zeros], axis=0)),
            )
            one = product[base : base + HALF, 0:LANES]
            two = jnp.concatenate([product[base + HALF : base + ROWS, 0:LANES], packed], axis=0)
            owner = 8 * part + inner
            keep_ref[owner] = jnp.where(first_core, one, two)
            send_ref[owner] = jnp.where(first_core, two, one).astype(bf16)


def back_kernel(grads_ref, weight_ref, input_grad_ref):
    tall = grads_ref[...]
    for part in range(10):
        cols = slice(256 * part, 256 * part + 256)
        product = lax.dot_general(tall, weight_ref[cols, :], NT, preferred_element_type=f32)
        input_grad_ref[:, cols] = (product[0:TOK] + product[TOK:]).astype(bf16)


def finish_kernel(parts_ref, bc_ref, dt_ref):
    one = parts_ref[0].astype(f32)
    two = parts_ref[1].astype(f32)
    for place in range(2, SEQ, 2):
        one = one + parts_ref[place].astype(f32)
        two = two + parts_ref[place + 1].astype(f32)
    scale = 1.0 / math.sqrt(SEQ * DP * TOK)
    bc = jnp.concatenate([one, two[0:REST]], axis=0) * scale
    bc_ref[...] = mm_exact(bc, interleave((LANES, LANES), 1))
    packed = two[REST:HALF] * scale
    head, lane = iota((HEADS, LANES), 0), iota((HEADS, LANES), 1)
    for k in range(3):
        rows = min(32, ROWS - 32 * k)
        dt_ref[:, 32 * k : 32 * k + rows] = mm_exact(
            ones_where(lane == head + 40 * k), packed[0:rows], NT
        )


def call(kernel, name, out_shape, scalars, arrays, scratch=(), flops=0, bytes_accessed=0):
    smem = pl.BlockSpec(memory_space=pltpu.SMEM)
    vmem = pl.BlockSpec(memory_space=pltpu.VMEM)
    return pl.pallas_call(
        kernel,
        name=name,
        out_shape=out_shape,
        in_specs=[smem] * len(scalars) + [vmem] * len(arrays),
        out_specs=jax.tree.map(lambda _: vmem, out_shape),
        scratch_shapes=scratch,
        compiler_params=pltpu.CompilerParams(vmem_limit_bytes=20 << 20),
        cost_estimate=pl.CostEstimate(
            flops=flops, bytes_accessed=bytes_accessed, transcendentals=0
        ),
    )(*scalars, *arrays)


def shape(dims, dtype):
    return jax.ShapeDtypeStruct(dims, dtype)


SWAP = [(place, place ^ 1) for place in range(SEQ)]


def body(features, head_inputs, out_grad, bc_weight, dt_weight, dt_bias, decay_rate, skip_gain):
    core = (lax.axis_index("seq") & 1).astype(jnp.int32).reshape(1)
    feats, x, g = features[0], head_inputs[0], out_grad[0]
    bias, rate, skip = dt_bias[None], decay_rate[None], skip_gain[None]
    square = shape((TOK, LANES), f32)
    chunks = shape((DP, HALF, LANES), bf16)

    sent = call(pack_kernel, "pack", chunks, [core], [bc_weight, dt_weight.T])
    mine = lax.all_to_all(sent, "dp", 0, 0, tiled=True)
    turned = call(turn_kernel, "turn", shape((WIDE, TOK), bf16), [], [feats], bytes_accessed=2_000_000)
    other = lax.ppermute(mine, "seq", SWAP)
    weight, proj, pre, cum, local = call(
        first_kernel,
        "first",
        (shape((WIDE, 2 * LANES), bf16), square, square, square, shape((SEQ, 168, LANES), bf16)),
        [core],
        [mine, other, feats, x, g, bias, rate],
    )
    gathered = lax.all_to_all(local, "seq", 0, 0, tiled=True)
    half = (shape((TOK, WIDE // 2), f32), square, square, square)
    cost = dict(flops=200_000_000, bytes_accessed=3_000_000)
    left, across, own, rows = call(
        partial(inside_kernel, 0, True), "inside_left", half, [], [proj, pre, cum, x, g], **cost
    )
    entering = call(
        chain_kernel, "chain", shape((SEQ, 160, LANES), bf16), [], [gathered, across[0:8]]
    )
    carried = lax.all_to_all(entering, "seq", 0, 0, tiled=True)
    right, across, own, rows = call(
        partial(inside_kernel, PAIRS // 2, False), "inside_right", half, [],
        [proj, pre, cum, x, g, across, own, rows], **cost,
    )
    grads, head_grad, keep, send = call(
        last_kernel,
        "last",
        (
            shape((2 * TOK, 2 * LANES), bf16),
            shape((TOK, WIDE), bf16),
            shape((DP, HALF, LANES), f32),
            chunks,
        ),
        [core],
        [carried, proj, pre, cum, left, right, across, own, rows, turned, x, g, rate, skip],
    )
    paired = (keep + lax.ppermute(send, "seq", SWAP).astype(f32)).astype(bf16)
    owned = lax.all_to_all(paired, "dp", 0, 0, tiled=True)
    input_grad = call(
        back_kernel, "back", shape((TOK, WIDE), bf16), [], [grads, weight],
        flops=340_000_000, bytes_accessed=3_000_000,
    )
    owned = jnp.sum(owned.astype(f32), axis=0)
    parts = lax.all_gather(owned, "seq")
    bc_grad, dt_grad = call(
        finish_kernel, "finish", (shape((ROWS, LANES), f32), shape((HEADS, ROWS), f32)), [], [parts]
    )
    return input_grad[None], head_grad[None], bc_grad, dt_grad.T


def solution(mesh):
    in_specs = (
        P("dp", "seq", None),
        P("dp", "seq", None),
        P("dp", "seq", None),
        P("dp", None),
        P("dp", None),
        P(),
        P(),
        P(),
    )
    out_specs = (P("dp", "seq", None), P("dp", "seq", None), P("dp", None), P("dp", None))
    return jax.shard_map(body, mesh=mesh, in_specs=in_specs, out_specs=out_specs, check_vma=False)
```

```python
import math

import jax
import jax.numpy as jnp
from jax import lax
from jax.experimental import pallas as pl
from jax.experimental.pallas import tpu as pltpu
from jax.sharding import PartitionSpec as P

bf16, f32 = jnp.bfloat16, jnp.float32
highest = lax.Precision.HIGHEST

HEADS = 40
PAIRS = 20
TOK = 128
WIDE = 2560
ROWS = 80
DP = 32
SEQ = 16
HALF = 56
REST = 24
LANES = 128

NN = (((1,), (0,)), ((), ()))
NT = (((1,), (1,)), ((), ()))
TN = (((0,), (0,)), ((), ()))


def iota(shape, axis):
    return lax.broadcasted_iota(jnp.int32, shape, axis)


def ones_where(mask, dtype=f32):
    return jnp.where(mask, 1.0, 0.0).astype(dtype)


def mm(a, b, dims=NN):
    return lax.dot_general(a.astype(bf16), b.astype(bf16), dims, preferred_element_type=f32)


def high_low(value):
    high = value.astype(bf16)
    return high, (value - high.astype(f32)).astype(bf16)


def mm_exact(a, b, dims=NN):
    return lax.dot_general(a, b, dims, precision=highest, preferred_element_type=f32)


def head_of_lane(lane):
    return lane - jnp.where(lane >= 40, 40, 0) - jnp.where(lane >= 80, 40, 0)


def interleave(shape, source_axis):
    source, target = iota(shape, source_axis), iota(shape, 1 - source_axis)
    low = target & 7
    wanted = 4 * (target >> 3) + low + jnp.where(low >= 4, 60, 0)
    return ones_where(source == wanted)


def triple(row):
    place = ones_where(iota((HEADS, LANES), 0) == head_of_lane(iota((HEADS, LANES), 1)))
    return mm_exact(jnp.broadcast_to(row, (8, HEADS)), place)[0:1]


def split(value):
    lane = iota(value.shape, 1)
    first = value.astype(bf16).astype(f32)
    rest = value - first
    second = rest.astype(bf16).astype(f32)
    third = rest - second
    return jnp.where(lane < 40, first, jnp.where(lane < 80, second, third)).astype(bf16)


def spread_matrix(pair, pairs=1):
    k, lane = iota((LANES, LANES * pairs), 0), iota((LANES, LANES * pairs), 1)
    return ones_where(head_of_lane(k) == 2 * pair + (lane >> 6), bf16)


def gather_matrix(pair, pairs=1):
    lane, k = iota((LANES * pairs, LANES), 0), iota((LANES * pairs, LANES), 1)
    return ones_where(head_of_lane(k) == 2 * pair + (lane >> 6), bf16)


def pack_kernel(core_ref, bc_ref, dt_ref, out_ref):
    bc = mm(bc_ref[...], interleave((LANES, LANES), 0))
    row, lane = iota((HEADS, LANES), 0), iota((HEADS, LANES), 1)
    dt = [mm(dt_ref[...], ones_where(lane == row + 40 * k), TN) for k in range(3)]
    last = jnp.concatenate([dt[2][64:80], jnp.zeros((16, LANES), f32)], axis=0)
    packed = dt[0][0:32] + dt[1][32:64] + last
    second = jnp.concatenate([bc[HALF:ROWS], packed], axis=0)
    value = jnp.where(core_ref[0] == 0, bc[0:HALF], second).astype(bf16)
    for owner in range(DP):
        out_ref[owner] = value


def turn_kernel(feat_ref, out_ref):
    for part in range(PAIRS):
        rows = slice(LANES * part, LANES * part + LANES)
        out_ref[rows, :] = feat_ref[:, rows].T


def first_kernel(
    core_ref, mine_ref, other_ref, feat_hbm, x_ref, g_ref, bias_ref, rate_ref,
    weight_hbm, small_ref, state_ref, weight_ref, feat_ref, sems,
):
    fetch = pltpu.make_async_copy(feat_hbm, feat_ref, sems.at[0])
    fetch.start()
    lane16 = iota((16, LANES), 1)
    group = [
        ones_where((lane16 >= 40 * k) & (lane16 < 40 * k + 40), bf16) for k in range(3)
    ]

    def assemble(one_ref, two_ref):
        for owner in range(DP):
            base = ROWS * owner
            weight_ref[base : base + HALF, 0:LANES] = one_ref[owner]
            weight_ref[base + HALF : base + ROWS, 0:LANES] = two_ref[owner, 0:REST, :]
            low, high = two_ref[owner, 24:40, :], two_ref[owner, 40:56, :]
            weight_ref[base : base + 16, LANES:] = low * group[0]
            weight_ref[base + 16 : base + 32, LANES:] = high * group[0]
            weight_ref[base + 32 : base + 48, LANES:] = low * group[1]
            weight_ref[base + 48 : base + 64, LANES:] = high * group[1]
            weight_ref[base + 64 : base + 80, LANES:] = low * group[2]

    core = core_ref[0]

    @pl.when(core == 0)
    def _():
        assemble(mine_ref, other_ref)

    @pl.when(core != 0)
    def _():
        assemble(other_ref, mine_ref)

    store = pltpu.make_async_copy(weight_ref, weight_hbm, sems.at[1])
    store.start()
    fetch.wait()
    both = lax.dot_general(feat_ref[...], weight_ref[...], NN, preferred_element_type=f32)
    proj = both[:, 0:LANES]
    row, lane = iota((LANES, LANES), 0), iota((LANES, LANES), 1)
    head_row, head_lane = head_of_lane(row), head_of_lane(lane)
    fold = ones_where((head_row == head_lane) & (head_lane < HEADS))
    pre = mm_exact(both[:, LANES:], fold) + triple(bias_ref[...])
    step = jnp.maximum(pre, 0.0) + jnp.log1p(jnp.exp(-jnp.abs(pre)))
    cum = mm_exact(ones_where(row >= lane), -triple(rate_ref[...]) * step)
    small_ref[0] = proj
    small_ref[1] = pre
    small_ref[2] = cum
    total = cum[TOK - 1 : TOK]
    stacked = jnp.concatenate(
        [split(step * jnp.exp(total - cum)), split(jnp.exp(cum))], axis=0
    )
    turned_high, turned_low = high_low(proj.T)
    both_turned = jnp.concatenate([turned_high, turned_low], axis=0)
    forward = (iota((LANES, 2 * LANES), 0) & 7) < 4

    for two in range(PAIRS // 2):
        cols = slice(256 * two, 256 * two + 256)
        wide = lax.dot_general(
            stacked, spread_matrix(2 * two, 2), NN, preferred_element_type=f32
        )
        ending = high_low(x_ref[:, cols].astype(f32) * wide[0:TOK])
        weighted = high_low(g_ref[:, cols].astype(f32) * wide[TOK:])

        def product(halves):
            value = mm(both_turned, halves[0])
            return value[0:LANES] + (value[LANES:] + mm(turned_high, halves[1]))

        chosen = jnp.where(forward, product(ending), product(weighted))
        value = jnp.concatenate(
            [chosen[:, k * LANES : k * LANES + LANES].reshape(SEQ, 8, LANES) for k in range(2)],
            axis=1,
        )
        state_ref[:, 16 * two : 16 * two + 16, :] = value.astype(bf16)
    decay = split(jnp.broadcast_to(total, (8, LANES)))
    for owner in range(SEQ):
        state_ref[owner, 160:168, :] = decay
    store.wait()


def chain_kernel(state_ref, out_ref):
    row16 = iota((16, LANES), 0)
    logs = jnp.zeros((16, LANES), f32)
    for place in range(SEQ):
        line = state_ref[place, 160:168, :].astype(f32)
        logs = logs + jnp.where(row16 == place, jnp.concatenate([line, line], axis=0), 0.0)
    logs = logs.astype(bf16)
    forward = (row16 & 7) < 4
    for two in range(PAIRS // 2):
        rows = slice(16 * two, 16 * two + 16)
        factor = [
            jnp.exp(
                lax.dot_general(
                    logs, spread_matrix(2 * two + k), NN, preferred_element_type=f32
                )
            )
            for k in range(2)
        ]

        def decay(place):
            return jnp.concatenate(
                [jnp.broadcast_to(factor[k][place : place + 1], (8, LANES)) for k in range(2)],
                axis=0,
            )

        values = [state_ref[place, rows, :].astype(f32) for place in range(SEQ)]
        decays = [decay(place) for place in range(SEQ)]
        ahead = [jnp.zeros((16, LANES), f32)]
        for place in range(SEQ - 1):
            ahead.append(ahead[-1] * decays[place] + values[place])
        back = jnp.zeros((16, LANES), f32)
        for place in range(SEQ - 1, -1, -1):
            out_ref[place, rows, :] = jnp.where(forward, ahead[place], back).astype(bf16)
            back = back * decays[place] + values[place]


def softplus(pre):
    return jnp.maximum(pre, 0.0) + jnp.log1p(jnp.exp(-jnp.abs(pre)))


def inside_kernel(small_ref, x_ref, g_ref, scaled_hbm, sums_ref, scaled_ref, sem):
    proj, cum = small_ref[0], small_ref[2]
    step = softplus(small_ref[1])
    row, lane = iota((LANES, LANES), 0), iota((LANES, LANES), 1)
    low = (lane & 7) < 4
    b_low = jnp.where(low, proj, 0.0)
    c_low = jnp.where(low, pltpu.roll(proj, LANES - 4, 1), 0.0)
    meet = mm_exact(b_low, c_low, NT)
    causal = lane >= row
    cum_turned = cum.T
    lane_head = head_of_lane(lane)
    across = jnp.zeros((TOK, TOK), f32)
    own = jnp.zeros((TOK, LANES), f32)
    sums_ref[2] = jnp.zeros((LANES, TOK), f32)
    first_half = ones_where(lane < 64, bf16)
    second_half = ones_where(lane >= 64, bf16)
    for pair in range(PAIRS):
        cols = slice(LANES * pair, LANES * pair + LANES)
        x, g = x_ref[:, cols], g_ref[:, cols]
        mixed, parts = [], []
        for which, half in enumerate((first_half, second_half)):
            head = 2 * pair + which
            g_half = g * half
            outer = lax.dot_general(x, g_half, NT, preferred_element_type=f32)
            gap = cum_turned[head : head + 1, :] - cum[:, head : head + 1]
            weight = jnp.exp(jnp.where(causal, gap, -1e30))
            step_col = step[:, head : head + 1]
            spot = outer * weight
            across = across + spot * step_col
            product = spot * meet
            own = jnp.where(lane_head == head, jnp.sum(product, axis=1, keepdims=True), own)
            sums_ref[2, head : head + 1, :] = jnp.sum(product * step_col, axis=0, keepdims=True)
            mixed.append((meet * weight).astype(bf16))
            parts.append(g_half)
        scaled_ref[:, cols] = lax.dot_general(
            jnp.concatenate(mixed, axis=1), jnp.concatenate(parts, axis=0), NN,
            preferred_element_type=f32,
        )
    sums_ref[0] = across
    sums_ref[1] = own
    store = pltpu.make_async_copy(scaled_ref, scaled_hbm, sem)
    store.start()
    store.wait()


def last_kernel(
    core_ref, carried_ref, small_ref, scaled_hbm, inner_ref, turned_ref, x_ref, g_ref,
    rate_ref, skip_ref,
    grads_ref, head_grad_ref, keep_ref, send_ref,
    scaled_ref, state_all, lines_all, terms_all, select_all, sem,
):
    fetch = pltpu.make_async_copy(scaled_hbm, scaled_ref, sem)
    fetch.start()
    proj, pre, cum = small_ref[0], small_ref[1], small_ref[2]
    step = softplus(pre)
    total = cum[TOK - 1 : TOK]
    row, lane = iota((LANES, LANES), 0), iota((LANES, LANES), 1)
    low = (lane & 7) < 4
    c_low = jnp.where(low, pltpu.roll(proj, LANES - 4, 1), 0.0)
    b_high = jnp.where(low, 0.0, pltpu.roll(proj, 4, 1))
    left = jnp.concatenate([c_low, b_high], axis=0)
    left = jnp.concatenate(high_low(left), axis=0)
    stacked = jnp.concatenate(
        [
            split(step),
            split(jnp.exp(total - cum)),
            split(jnp.exp(cum)),
            split(jnp.broadcast_to(triple(skip_ref[...]), (16, LANES))),
        ],
        axis=0,
    )
    low_rows = (iota((LANES, 2 * LANES), 0) & 7) < 4
    for two in range(PAIRS // 2):
        cols = slice(256 * two, 256 * two + 256)
        later_cols = slice(WIDE + 256 * two, WIDE + 256 * two + 256)
        chunk = carried_ref[:, 16 * two : 16 * two + 16, :].astype(f32)
        state = jnp.concatenate(
            [chunk[:, 8 * k : 8 * k + 8, :].reshape(LANES, LANES) for k in range(2)], axis=1
        )
        state_b = state.astype(bf16)
        state_all[:, cols] = state_b
        select_all[cols, :] = gather_matrix(2 * two, 2)
        wide = lax.dot_general(
            stacked, spread_matrix(2 * two, 2), NN, preferred_element_type=f32
        )
        step_w, end_w, start_w = wide[0:TOK], wide[TOK : 2 * TOK], wide[2 * TOK : 3 * TOK]
        skip_w = wide[3 * TOK : 3 * TOK + 1]
        x, g = x_ref[:, cols].astype(f32), g_ref[:, cols].astype(f32)
        weighted = g * start_w
        ending = x * end_w
        pushed = lax.dot_general(left, state_b, NN, preferred_element_type=f32)
        pushed = pushed[0 : 2 * TOK] + pushed[2 * TOK :]
        out, reach = pushed[0:TOK], pushed[TOK:]
        high, low_part = high_low(jnp.concatenate([weighted, ending * step_w], axis=0))
        lines_all[:, cols] = high
        lines_all[:, later_cols] = low_part
        pairing = jnp.where(low_rows, state * pltpu.roll(state, LANES - 4, 0), 0.0)
        pairing = jnp.sum(pairing.reshape(SEQ, 8, 2 * LANES), axis=0)
        pairing = jnp.concatenate([pairing, jnp.zeros((8, 2 * LANES), f32)], axis=0)
        high, low_part = high_low(
            jnp.concatenate([weighted * out, ending * reach, pairing], axis=0)
        )
        terms_all[:, cols] = high
        terms_all[:, later_cols] = low_part
        if two == 0:
            fetch.wait()
        whole = scaled_ref[:, cols] + end_w * reach
        head_grad_ref[:, cols] = (g * skip_w + step_w * whole).astype(bf16)

    def both_parts(ref, right, dims):
        return lax.dot_general(
            ref[:, 0:WIDE], right, dims, preferred_element_type=f32
        ) + lax.dot_general(ref[:, WIDE:], right, dims, preferred_element_type=f32)

    crossed = both_parts(lines_all, state_all[...], NT)
    sums = both_parts(terms_all, select_all[...], NN)
    through, reached = sums[0:TOK], sums[TOK : 2 * TOK]
    paired = jnp.sum(sums[2 * TOK : 2 * TOK + 8], axis=0, keepdims=True)
    own = inner_ref[1]
    lane_head = head_of_lane(lane)
    later = mm_exact(inner_ref[2].T, ones_where((row == lane_head) & (row < HEADS)))
    decay_grad = (
        mm_exact(ones_where(lane >= row), later - step * own + through)
        + mm_exact(ones_where(lane < row), step * reached)
        + jnp.exp(total) * paired
    )
    step_grad = own + reached - triple(rate_ref[...]) * decay_grad
    pre_grad = step_grad * jax.nn.sigmoid(pre)
    pre_grad = jnp.where(lane < 3 * HEADS, pre_grad, 0.0)
    across = inner_ref[0]
    bc_grad = mm_exact(across, c_low) + mm_exact(across.T, b_high)
    bc_grad = bc_grad + jnp.where(
        low, pltpu.roll(crossed[TOK:], LANES - 4, 1), pltpu.roll(crossed[0:TOK], 4, 1)
    )
    grads = high_low(jnp.concatenate([bc_grad, pre_grad], axis=1))
    tall, flat = jnp.concatenate(grads, axis=0), jnp.concatenate(grads, axis=1)
    grads_ref[...] = tall
    first_core = core_ref[0] == 0
    lane32 = iota((32, LANES), 1)
    zeros = jnp.zeros((16, LANES), f32)
    for part in range(4):
        rows = slice(640 * part, 640 * part + 640)
        product = lax.dot_general(turned_ref[rows, :], flat, NN, preferred_element_type=f32)
        product = product[:, 0 : 2 * LANES] + product[:, 2 * LANES :]
        for inner in range(8):
            base = ROWS * inner
            dt = product[base : base + ROWS, LANES:]
            packed = jnp.where(
                lane32 < 40,
                dt[0:32],
                jnp.where(lane32 < 80, dt[32:64], jnp.concatenate([dt[64:80], zeros], axis=0)),
            )
            one = product[base : base + HALF, 0:LANES]
            two = jnp.concatenate([product[base + HALF : base + ROWS, 0:LANES], packed], axis=0)
            owner = 8 * part + inner
            keep_ref[owner] = jnp.where(first_core, one, two)
            send_ref[owner] = jnp.where(first_core, two, one).astype(bf16)


def back_kernel(grads_ref, weight_ref, input_grad_ref, token_ref):
    token_ref[...] = jnp.zeros_like(token_ref)
    tall = grads_ref[...]
    for part in range(10):
        cols = slice(256 * part, 256 * part + 256)
        product = lax.dot_general(tall, weight_ref[cols, :], NT, preferred_element_type=f32)
        input_grad_ref[:, cols] = (product[0:TOK] + product[TOK:]).astype(bf16)


def join_kernel(keep_ref, other_ref, token_ref, out_ref):
    for owner in range(DP):
        out_ref[owner] = (keep_ref[owner] + other_ref[owner].astype(f32)).astype(bf16)


def finish_kernel(parts_ref, bc_ref, dt_ref):
    one = parts_ref[0].astype(f32)
    two = parts_ref[1].astype(f32)
    for place in range(2, SEQ, 2):
        one = one + parts_ref[place].astype(f32)
        two = two + parts_ref[place + 1].astype(f32)
    scale = 1.0 / math.sqrt(SEQ * DP * TOK)
    bc = jnp.concatenate([one, two[0:REST]], axis=0) * scale
    bc_ref[...] = mm_exact(bc, interleave((LANES, LANES), 1))
    packed = two[REST:HALF] * scale
    head, lane = iota((HEADS, LANES), 0), iota((HEADS, LANES), 1)
    for k in range(3):
        rows = min(32, ROWS - 32 * k)
        dt_ref[:, 32 * k : 32 * k + rows] = mm_exact(
            ones_where(lane == head + 40 * k), packed[0:rows], NT
        )


def call(kernel, name, out_shape, scalars, arrays, in_hbm=(), out_hbm=(), **options):
    smem = pl.BlockSpec(memory_space=pltpu.SMEM)
    vmem = pl.BlockSpec(memory_space=pltpu.VMEM)
    hbm = pl.BlockSpec(memory_space=pltpu.HBM)
    flops, moved = options.pop("cost", (0, 0))
    several = isinstance(out_shape, tuple)
    if out_hbm:
        out_shape = tuple(
            pltpu.HBM(part.shape, part.dtype) if k in out_hbm else part
            for k, part in enumerate(out_shape)
        )
    arrays = [
        pltpu.with_memory_space_constraint(part, pltpu.HBM) if k in in_hbm else part
        for k, part in enumerate(arrays)
    ]
    out_specs = [hbm if k in out_hbm else vmem for k in range(len(out_shape))] if several else vmem
    return pl.pallas_call(
        kernel,
        name=name,
        out_shape=out_shape,
        in_specs=[smem] * len(scalars)
        + [hbm if k in in_hbm else vmem for k in range(len(arrays))],
        out_specs=tuple(out_specs) if several else out_specs,
        scratch_shapes=options.pop("scratch", ()),
        compiler_params=pltpu.CompilerParams(vmem_limit_bytes=40 << 20),
        cost_estimate=pl.CostEstimate(flops=flops, bytes_accessed=moved, transcendentals=0),
    )(*scalars, *arrays)


def shape(dims, dtype):
    return jax.ShapeDtypeStruct(dims, dtype)


SWAP = [(place, place ^ 1) for place in range(SEQ)]


def body(features, head_inputs, out_grad, bc_weight, dt_weight, dt_bias, decay_rate, skip_gain):
    core = (lax.axis_index("seq") & 1).astype(jnp.int32).reshape(1)
    feats, x, g = features[0], head_inputs[0], out_grad[0]
    bias, rate, skip = dt_bias[None], decay_rate[None], skip_gain[None]
    chunks = shape((DP, HALF, LANES), bf16)
    three = shape((3, TOK, LANES), f32)
    dma = pltpu.SemaphoreType.DMA

    sent = call(pack_kernel, "pack", chunks, [core], [bc_weight, dt_weight.T])
    mine = lax.all_to_all(sent, "dp", 0, 0, tiled=True)
    other = lax.ppermute(mine, "seq", SWAP)
    weight, small, local = call(
        first_kernel,
        "first",
        (shape((WIDE, 2 * LANES), bf16), three, shape((SEQ, 168, LANES), bf16)),
        [core],
        [mine, other, feats, x, g, bias, rate],
        in_hbm=(2,),
        out_hbm=(0,),
        scratch=[
            pltpu.VMEM((WIDE, 2 * LANES), bf16),
            pltpu.VMEM((TOK, WIDE), bf16),
            dma((2,)),
        ],
    )
    gathered = lax.all_to_all(local, "seq", 0, 0, tiled=True)
    entering = call(chain_kernel, "chain", shape((SEQ, 160, LANES), bf16), [], [gathered])
    carried = lax.all_to_all(entering, "seq", 0, 0, tiled=True)
    scaled, inner = call(
        inside_kernel,
        "inside",
        (shape((TOK, WIDE), f32), three),
        [],
        [small, x, g],
        out_hbm=(0,),
        scratch=[pltpu.VMEM((TOK, WIDE), f32), dma],
        cost=(400_000_000, 4_000_000),
    )
    turned = call(turn_kernel, "turn", shape((WIDE, TOK), bf16), [], [feats], cost=(0, 2_000_000))
    grads, head_grad, keep, send = call(
        last_kernel,
        "last",
        (
            shape((2 * TOK, 2 * LANES), bf16),
            shape((TOK, WIDE), bf16),
            shape((DP, HALF, LANES), f32),
            chunks,
        ),
        [core],
        [carried, small, scaled, inner, turned, x, g, rate, skip],
        in_hbm=(2,),
        scratch=[
            pltpu.VMEM((TOK, WIDE), f32),
            pltpu.VMEM((LANES, WIDE), bf16),
            pltpu.VMEM((2 * TOK, 2 * WIDE), bf16),
            pltpu.VMEM((2 * TOK + 16, 2 * WIDE), bf16),
            pltpu.VMEM((WIDE, LANES), bf16),
            dma,
        ],
    )
    other = lax.ppermute(send, "seq", SWAP)
    input_grad, token = call(
        back_kernel,
        "back",
        (shape((TOK, WIDE), bf16), shape((8, LANES), f32)),
        [],
        [grads, weight],
        cost=(340_000_000, 3_000_000),
    )
    paired = call(join_kernel, "join", chunks, [], [keep, other, token])
    owned = lax.all_to_all(paired, "dp", 0, 0, tiled=True)
    owned = jnp.sum(owned.astype(f32), axis=0)
    parts = lax.all_gather(owned, "seq")
    bc_grad, dt_grad = call(
        finish_kernel, "finish", (shape((ROWS, LANES), f32), shape((HEADS, ROWS), f32)), [], [parts]
    )
    return input_grad[None], head_grad[None], bc_grad, dt_grad.T


def solution(mesh):
    in_specs = (
        P("dp", "seq", None),
        P("dp", "seq", None),
        P("dp", "seq", None),
        P("dp", None),
        P("dp", None),
        P(),
        P(),
        P(),
    )
    out_specs = (P("dp", "seq", None), P("dp", "seq", None), P("dp", None), P("dp", None))
    return jax.shard_map(body, mesh=mesh, in_specs=in_specs, out_specs=out_specs, check_vma=False)
```

```python
import math

import jax
import jax.numpy as jnp
from jax import lax
from jax.experimental import pallas as pl
from jax.experimental.pallas import tpu as pltpu
from jax.sharding import PartitionSpec as P

bf16, f32 = jnp.bfloat16, jnp.float32
highest = lax.Precision.HIGHEST

HEADS = 40
PAIRS = 20
TOK = 128
WIDE = 2560
ROWS = 80
DP = 32
SEQ = 16
CHIPS = 8
STATE = 64
HALF = 56
REST = 24
LANES = 128

NN = (((1,), (0,)), ((), ()))
NT = (((1,), (1,)), ((), ()))
TN = (((0,), (0,)), ((), ()))


def iota(shape, axis):
    return lax.broadcasted_iota(jnp.int32, shape, axis)


def ones_where(mask, dtype=f32):
    return jnp.where(mask, 1.0, 0.0).astype(dtype)


def mm(a, b, dims=NN):
    return lax.dot_general(a.astype(bf16), b.astype(bf16), dims, preferred_element_type=f32)


def high_low(value):
    high = value.astype(bf16)
    return high, (value - high.astype(f32)).astype(bf16)


def mm_exact(a, b, dims=NN):
    return lax.dot_general(a, b, dims, precision=highest, preferred_element_type=f32)


def head_of_lane(lane):
    return lane - jnp.where(lane >= 40, 40, 0) - jnp.where(lane >= 80, 40, 0)


def triple(row):
    place = ones_where(iota((HEADS, LANES), 0) == head_of_lane(iota((HEADS, LANES), 1)))
    return mm_exact(jnp.broadcast_to(row, (8, HEADS)), place)[0:1]


def split(value):
    lane = iota(value.shape, 1)
    first = value.astype(bf16).astype(f32)
    rest = value - first
    second = rest.astype(bf16).astype(f32)
    third = rest - second
    return jnp.where(lane < 40, first, jnp.where(lane < 80, second, third)).astype(bf16)


def spread_matrix(pair, pairs=1):
    k, lane = iota((LANES, LANES * pairs), 0), iota((LANES, LANES * pairs), 1)
    return ones_where(head_of_lane(k) == 2 * pair + (lane >> 6), bf16)


def gather_matrix(pair, pairs=1):
    lane, k = iota((LANES * pairs, LANES), 0), iota((LANES * pairs, LANES), 1)
    return ones_where(head_of_lane(k) == 2 * pair + (lane >> 6), bf16)


def pack_kernel(core_ref, bc_ref, dt_ref, out_ref):
    bc = bc_ref[...].astype(f32)
    row, lane = iota((HEADS, LANES), 0), iota((HEADS, LANES), 1)
    dt = [mm(dt_ref[...], ones_where(lane == row + 40 * k), TN) for k in range(3)]
    last = jnp.concatenate([dt[2][64:80], jnp.zeros((16, LANES), f32)], axis=0)
    packed = dt[0][0:32] + dt[1][32:64] + last
    second = jnp.concatenate([bc[HALF:ROWS], packed], axis=0)
    value = jnp.where(core_ref[0] == 0, bc[0:HALF], second).astype(bf16)
    for owner in range(DP):
        out_ref[owner] = value


def turn_kernel(feat_ref, out_ref):
    for part in range(PAIRS):
        rows = slice(LANES * part, LANES * part + LANES)
        out_ref[rows, :] = feat_ref[:, rows].T


def first_kernel(
    core_ref, mine_ref, other_ref, feat_hbm, x_ref, g_ref, bias_ref, rate_ref,
    weight_hbm, small_ref, held_ref, sent_ref, weight_ref, feat_ref, sems,
):
    fetch = pltpu.make_async_copy(feat_hbm, feat_ref, sems.at[0])
    fetch.start()
    lane16 = iota((16, LANES), 1)
    group = [
        ones_where((lane16 >= 40 * k) & (lane16 < 40 * k + 40), bf16) for k in range(3)
    ]

    def assemble(one_ref, two_ref):
        for owner in range(DP):
            base = ROWS * owner
            weight_ref[base : base + HALF, 0:LANES] = one_ref[owner]
            weight_ref[base + HALF : base + ROWS, 0:LANES] = two_ref[owner, 0:REST, :]
            low, high = two_ref[owner, 24:40, :], two_ref[owner, 40:56, :]
            weight_ref[base : base + 16, LANES:] = low * group[0]
            weight_ref[base + 16 : base + 32, LANES:] = high * group[0]
            weight_ref[base + 32 : base + 48, LANES:] = low * group[1]
            weight_ref[base + 48 : base + 64, LANES:] = high * group[1]
            weight_ref[base + 64 : base + 80, LANES:] = low * group[2]

    core = core_ref[0]

    @pl.when(core == 0)
    def _():
        assemble(mine_ref, other_ref)

    @pl.when(core != 0)
    def _():
        assemble(other_ref, mine_ref)

    store = pltpu.make_async_copy(weight_ref, weight_hbm, sems.at[1])
    store.start()
    fetch.wait()
    both = lax.dot_general(feat_ref[...], weight_ref[...], NN, preferred_element_type=f32)
    proj = both[:, 0:LANES]
    row, lane = iota((LANES, LANES), 0), iota((LANES, LANES), 1)
    head_row, head_lane = head_of_lane(row), head_of_lane(lane)
    fold = ones_where((head_row == head_lane) & (head_lane < HEADS))
    pre = mm_exact(both[:, LANES:], fold) + triple(bias_ref[...])
    step = jnp.maximum(pre, 0.0) + jnp.log1p(jnp.exp(-jnp.abs(pre)))
    cum = mm_exact(ones_where(row >= lane), -triple(rate_ref[...]) * step)
    small_ref[0] = proj
    small_ref[1] = pre
    small_ref[2] = cum
    total = cum[TOK - 1 : TOK]
    stacked = jnp.concatenate(
        [split(step * jnp.exp(total - cum)), split(jnp.exp(cum))], axis=0
    )
    turned_high, turned_low = high_low(proj.T)
    b_turned = jnp.concatenate([turned_high[0:STATE], turned_low[0:STATE]], axis=0)
    c_turned = jnp.concatenate([turned_high[STATE:], turned_low[STATE:]], axis=0)

    def product(turned, halves):
        value = mm(turned, halves[0])
        return value[0:STATE] + (value[STATE:] + mm(turned[0:STATE], halves[1]))

    for two in range(PAIRS // 2):
        cols = slice(256 * two, 256 * two + 256)
        rows = slice(16 * two, 16 * two + 16)
        wide = lax.dot_general(
            stacked, spread_matrix(2 * two, 2), NN, preferred_element_type=f32
        )
        onward = product(b_turned, high_low(x_ref[:, cols].astype(f32) * wide[0:TOK]))
        backward = product(c_turned, high_low(g_ref[:, cols].astype(f32) * wide[TOK:]))
        held_ref[:, rows, :] = to_chunks(jnp.where(core == 0, onward, backward))
        sent_ref[:, rows, :] = to_chunks(jnp.where(core == 0, backward, onward))
    for owner in range(CHIPS):
        sent_ref[owner, 160:168, :] = jnp.broadcast_to(total, (8, LANES))
    store.wait()


def to_chunks(value):
    parts = [value[:, LANES * k : LANES * k + LANES] for k in range(2)]
    return jnp.concatenate([part.reshape(CHIPS, 8, LANES) for part in parts], axis=1)


def chunk_factors(logs, two):
    wide = jnp.exp(
        lax.dot_general(logs, spread_matrix(2 * two, 2), NN, preferred_element_type=f32)
    )

    def factor(place):
        parts = [wide[place : place + 1, LANES * k : LANES * k + LANES] for k in range(2)]
        return jnp.concatenate([jnp.broadcast_to(part, (8, LANES)) for part in parts], axis=0)

    return factor


def chip_kernel(held_ref, other_ref, small_ref, out_ref):
    total_other = other_ref[0, 160:168, :]
    logs = split(jnp.concatenate([total_other, total_other], axis=0))
    for two in range(PAIRS // 2):
        rows = slice(16 * two, 16 * two + 16)
        factor = chunk_factors(logs, two)(0)
        for owner in range(CHIPS):
            value = other_ref[owner, rows, :] + held_ref[owner, rows, :] * factor
            out_ref[owner, rows, :] = value.astype(bf16)
    decay = split(total_other + small_ref[2, TOK - 1 : TOK, :])
    for owner in range(CHIPS):
        out_ref[owner, 160:168, :] = decay


def chain_kernel(core_ref, state_ref, out_ref):
    row16 = iota((16, LANES), 0)
    logs = jnp.zeros((16, LANES), f32)
    for place in range(CHIPS):
        line = state_ref[place, 160:168, :].astype(f32)
        logs = logs + jnp.where(row16 == place, jnp.concatenate([line, line], axis=0), 0.0)
    logs = logs.astype(bf16)
    forward = core_ref[0] == 0
    for two in range(PAIRS // 2):
        rows = slice(16 * two, 16 * two + 16)
        factor = chunk_factors(logs, two)
        values = [state_ref[place, rows, :].astype(f32) for place in range(CHIPS)]
        factors = [factor(place) for place in range(CHIPS)]
        ahead = [jnp.zeros((16, LANES), f32)]
        for place in range(CHIPS - 1):
            ahead.append(ahead[-1] * factors[place] + values[place])
        back = jnp.zeros((16, LANES), f32)
        for place in range(CHIPS - 1, -1, -1):
            out_ref[place, rows, :] = jnp.where(forward, ahead[place], back).astype(bf16)
            back = back * factors[place] + values[place]


def pass_kernel(carried_ref, held_ref, small_ref, after_ref, out_ref):
    logs = split(jnp.broadcast_to(small_ref[2, TOK - 1 : TOK, :], (16, LANES)))
    for two in range(PAIRS // 2):
        rows = slice(16 * two, 16 * two + 16)
        factor = chunk_factors(logs, two)(0)
        for owner in range(CHIPS):
            value = carried_ref[owner, rows, :].astype(f32) * factor + held_ref[owner, rows, :]
            out_ref[owner, rows, :] = value.astype(bf16)


def softplus(pre):
    return jnp.maximum(pre, 0.0) + jnp.log1p(jnp.exp(-jnp.abs(pre)))


def inside_kernel(small_ref, x_ref, g_ref, after_ref, scaled_hbm, sums_ref, scaled_ref, sem):
    proj, cum = small_ref[0], small_ref[2]
    step = softplus(small_ref[1])
    row, lane = iota((LANES, LANES), 0), iota((LANES, LANES), 1)
    low = lane < STATE
    b_low = jnp.where(low, proj, 0.0)
    c_low = jnp.where(low, pltpu.roll(proj, STATE, 1), 0.0)
    meet = mm_exact(b_low, c_low, NT)
    causal = lane >= row
    cum_turned = cum.T
    lane_head = head_of_lane(lane)
    across = jnp.zeros((TOK, TOK), f32)
    own = jnp.zeros((TOK, LANES), f32)
    sums_ref[2] = jnp.zeros((LANES, TOK), f32)
    first_half = ones_where(lane < 64, bf16)
    second_half = ones_where(lane >= 64, bf16)
    for pair in range(PAIRS):
        cols = slice(LANES * pair, LANES * pair + LANES)
        x, g = x_ref[:, cols], g_ref[:, cols]
        mixed, parts = [], []
        for which, half in enumerate((first_half, second_half)):
            head = 2 * pair + which
            g_half = g * half
            outer = lax.dot_general(x, g_half, NT, preferred_element_type=f32)
            gap = cum_turned[head : head + 1, :] - cum[:, head : head + 1]
            weight = jnp.exp(jnp.where(causal, gap, -1e30))
            step_col = step[:, head : head + 1]
            spot = outer * weight
            across = across + spot * step_col
            product = spot * meet
            own = jnp.where(lane_head == head, jnp.sum(product, axis=1, keepdims=True), own)
            sums_ref[2, head : head + 1, :] = jnp.sum(product * step_col, axis=0, keepdims=True)
            mixed.append((meet * weight).astype(bf16))
            parts.append(g_half)
        scaled_ref[:, cols] = lax.dot_general(
            jnp.concatenate(mixed, axis=1), jnp.concatenate(parts, axis=0), NN,
            preferred_element_type=f32,
        )
    sums_ref[0] = across
    sums_ref[1] = own
    store = pltpu.make_async_copy(scaled_ref, scaled_hbm, sem)
    store.start()
    store.wait()


def last_kernel(
    core_ref, carried_ref, other_ref, small_ref, scaled_hbm, inner_ref, turned_ref, x_ref, g_ref,
    rate_ref, skip_ref,
    grads_ref, head_grad_ref, keep_ref, send_ref,
    scaled_ref, state_all, lines_all, terms_all, select_all, sem,
):
    fetch = pltpu.make_async_copy(scaled_hbm, scaled_ref, sem)
    fetch.start()
    proj, pre, cum = small_ref[0], small_ref[1], small_ref[2]
    step = softplus(pre)
    total = cum[TOK - 1 : TOK]
    row, lane = iota((LANES, LANES), 0), iota((LANES, LANES), 1)
    low = lane < STATE
    proj_swapped = pltpu.roll(proj, STATE, 1)
    c_low = jnp.where(low, proj_swapped, 0.0)
    b_high = jnp.where(low, 0.0, proj_swapped)
    first_core = core_ref[0] == 0
    left = jnp.concatenate([c_low, b_high], axis=0)
    left = jnp.concatenate(high_low(left), axis=0)
    stacked = jnp.concatenate(
        [
            split(step),
            split(jnp.exp(total - cum)),
            split(jnp.exp(cum)),
            split(jnp.broadcast_to(triple(skip_ref[...]), (16, LANES))),
        ],
        axis=0,
    )

    def state_rows(chunk):
        parts = [chunk[:, 8 * k : 8 * k + 8, :].reshape(STATE, LANES) for k in range(2)]
        return jnp.concatenate(parts, axis=1)

    for two in range(PAIRS // 2):
        cols = slice(256 * two, 256 * two + 256)
        later_cols = slice(WIDE + 256 * two, WIDE + 256 * two + 256)
        rows = slice(16 * two, 16 * two + 16)
        mine = carried_ref[:, rows, :].astype(f32)
        other = other_ref[:, rows, :].astype(f32)
        state_in = state_rows(jnp.where(first_core, mine, other))
        state_grad = state_rows(jnp.where(first_core, other, mine))
        state_b = jnp.concatenate([state_in, state_grad], axis=0).astype(bf16)
        state_all[:, cols] = state_b
        select_all[cols, :] = gather_matrix(2 * two, 2)
        wide = lax.dot_general(
            stacked, spread_matrix(2 * two, 2), NN, preferred_element_type=f32
        )
        step_w, end_w, start_w = wide[0:TOK], wide[TOK : 2 * TOK], wide[2 * TOK : 3 * TOK]
        skip_w = wide[3 * TOK : 3 * TOK + 1]
        x, g = x_ref[:, cols].astype(f32), g_ref[:, cols].astype(f32)
        weighted = g * start_w
        ending = x * end_w
        pushed = lax.dot_general(left, state_b, NN, preferred_element_type=f32)
        pushed = pushed[0 : 2 * TOK] + pushed[2 * TOK :]
        out, reach = pushed[0:TOK], pushed[TOK:]
        high, low_part = high_low(jnp.concatenate([weighted, ending * step_w], axis=0))
        lines_all[:, cols] = high
        lines_all[:, later_cols] = low_part
        pairing = jnp.sum((state_in * state_grad).reshape(CHIPS, 8, 2 * LANES), axis=0)
        pairing = jnp.concatenate([pairing, jnp.zeros((8, 2 * LANES), f32)], axis=0)
        high, low_part = high_low(
            jnp.concatenate([weighted * out, ending * reach, pairing], axis=0)
        )
        terms_all[:, cols] = high
        terms_all[:, later_cols] = low_part
        if two == 0:
            fetch.wait()
        whole = scaled_ref[:, cols] + end_w * reach
        head_grad_ref[:, cols] = (g * skip_w + step_w * whole).astype(bf16)

    def both_parts(ref, right, dims):
        return lax.dot_general(
            ref[:, 0:WIDE], right, dims, preferred_element_type=f32
        ) + lax.dot_general(ref[:, WIDE:], right, dims, preferred_element_type=f32)

    crossed = both_parts(lines_all, state_all[...], NT)
    sums = both_parts(terms_all, select_all[...], NN)
    through, reached = sums[0:TOK], sums[TOK : 2 * TOK]
    paired = jnp.sum(sums[2 * TOK : 2 * TOK + 8], axis=0, keepdims=True)
    own = inner_ref[1]
    lane_head = head_of_lane(lane)
    later = mm_exact(inner_ref[2].T, ones_where((row == lane_head) & (row < HEADS)))
    decay_grad = (
        mm_exact(ones_where(lane >= row), later - step * own + through)
        + mm_exact(ones_where(lane < row), step * reached)
        + jnp.exp(total) * paired
    )
    step_grad = own + reached - triple(rate_ref[...]) * decay_grad
    pre_grad = step_grad * jax.nn.sigmoid(pre)
    pre_grad = jnp.where(lane < 3 * HEADS, pre_grad, 0.0)
    across = inner_ref[0]
    bc_grad = mm_exact(across, c_low) + mm_exact(across.T, b_high)
    bc_grad = bc_grad + jnp.where(
        low, pltpu.roll(crossed[TOK:], STATE, 1), pltpu.roll(crossed[0:TOK], STATE, 1)
    )
    grads = high_low(jnp.concatenate([bc_grad, pre_grad], axis=1))
    tall, flat = jnp.concatenate(grads, axis=0), jnp.concatenate(grads, axis=1)
    grads_ref[...] = tall
    lane32 = iota((32, LANES), 1)
    zeros = jnp.zeros((16, LANES), f32)
    for part in range(4):
        rows = slice(640 * part, 640 * part + 640)
        product = lax.dot_general(turned_ref[rows, :], flat, NN, preferred_element_type=f32)
        product = product[:, 0 : 2 * LANES] + product[:, 2 * LANES :]
        for inner in range(8):
            base = ROWS * inner
            dt = product[base : base + ROWS, LANES:]
            packed = jnp.where(
                lane32 < 40,
                dt[0:32],
                jnp.where(lane32 < 80, dt[32:64], jnp.concatenate([dt[64:80], zeros], axis=0)),
            )
            one = product[base : base + HALF, 0:LANES]
            two = jnp.concatenate([product[base + HALF : base + ROWS, 0:LANES], packed], axis=0)
            owner = 8 * part + inner
            keep_ref[owner] = jnp.where(first_core, one, two)
            send_ref[owner] = jnp.where(first_core, two, one).astype(bf16)


def back_kernel(grads_ref, weight_ref, input_grad_ref, token_ref):
    token_ref[...] = jnp.zeros_like(token_ref)
    tall = grads_ref[...]
    for part in range(10):
        cols = slice(256 * part, 256 * part + 256)
        product = lax.dot_general(tall, weight_ref[cols, :], NT, preferred_element_type=f32)
        input_grad_ref[:, cols] = (product[0:TOK] + product[TOK:]).astype(bf16)


def join_kernel(keep_ref, other_ref, token_ref, out_ref):
    for owner in range(DP):
        out_ref[owner] = (keep_ref[owner] + other_ref[owner].astype(f32)).astype(bf16)


def finish_kernel(parts_ref, bc_ref, dt_ref):
    one = parts_ref[0].astype(f32)
    two = parts_ref[1].astype(f32)
    for place in range(2, SEQ, 2):
        one = one + parts_ref[place].astype(f32)
        two = two + parts_ref[place + 1].astype(f32)
    scale = 1.0 / math.sqrt(SEQ * DP * TOK)
    bc = jnp.concatenate([one, two[0:REST]], axis=0) * scale
    bc_ref[...] = bc
    packed = two[REST:HALF] * scale
    head, lane = iota((HEADS, LANES), 0), iota((HEADS, LANES), 1)
    for k in range(3):
        rows = min(32, ROWS - 32 * k)
        dt_ref[:, 32 * k : 32 * k + rows] = mm_exact(
            ones_where(lane == head + 40 * k), packed[0:rows], NT
        )


def call(kernel, name, out_shape, scalars, arrays, in_hbm=(), out_hbm=(), after=(), **options):
    smem = pl.BlockSpec(memory_space=pltpu.SMEM)
    vmem = pl.BlockSpec(memory_space=pltpu.VMEM)
    hbm = pl.BlockSpec(memory_space=pltpu.HBM)
    flops, moved = options.pop("cost", (0, 0))
    several = isinstance(out_shape, tuple)
    if out_hbm:
        out_shape = tuple(
            pltpu.HBM(part.shape, part.dtype) if k in out_hbm else part
            for k, part in enumerate(out_shape)
        )
    arrays = [
        pltpu.with_memory_space_constraint(part, pltpu.HBM) if k in in_hbm else part
        for k, part in enumerate(arrays)
    ]
    out_specs = [hbm if k in out_hbm else vmem for k in range(len(out_shape))] if several else vmem
    return pl.pallas_call(
        kernel,
        name=name,
        out_shape=out_shape,
        in_specs=[smem] * len(scalars)
        + [hbm if k in in_hbm else vmem for k in range(len(arrays))]
        + [pl.BlockSpec(memory_space=pl.ANY)] * len(after),
        out_specs=tuple(out_specs) if several else out_specs,
        scratch_shapes=options.pop("scratch", ()),
        compiler_params=pltpu.CompilerParams(vmem_limit_bytes=40 << 20),
        cost_estimate=pl.CostEstimate(flops=flops, bytes_accessed=moved, transcendentals=0),
    )(*scalars, *arrays, *after)


def shape(dims, dtype):
    return jax.ShapeDtypeStruct(dims, dtype)


SWAP = [(place, place ^ 1) for place in range(SEQ)]
CORES = [[place for place in range(SEQ) if place % 2 == core] for core in range(2)]


def same_core_all_to_all(value):
    return lax.all_to_all(value, "seq", 0, 0, axis_index_groups=CORES, tiled=True)


def body(features, head_inputs, out_grad, bc_weight, dt_weight, dt_bias, decay_rate, skip_gain):
    core = (lax.axis_index("seq") & 1).astype(jnp.int32).reshape(1)
    feats, x, g = features[0], head_inputs[0], out_grad[0]
    bias, rate, skip = dt_bias[None], decay_rate[None], skip_gain[None]
    chunks = shape((DP, HALF, LANES), bf16)
    three = shape((3, TOK, LANES), f32)
    dma = pltpu.SemaphoreType.DMA

    sent = call(pack_kernel, "pack", chunks, [core], [bc_weight, dt_weight.T])
    mine = lax.all_to_all(sent, "dp", 0, 0, tiled=True)
    other = lax.ppermute(mine, "seq", SWAP)
    weight, small, held, leaving = call(
        first_kernel,
        "first",
        (
            shape((WIDE, 2 * LANES), bf16),
            three,
            shape((CHIPS, 160, LANES), f32),
            shape((CHIPS, 168, LANES), f32),
        ),
        [core],
        [mine, other, feats, x, g, bias, rate],
        in_hbm=(2,),
        out_hbm=(0,),
        scratch=[
            pltpu.VMEM((WIDE, 2 * LANES), bf16),
            pltpu.VMEM((TOK, WIDE), bf16),
            dma((2,)),
        ],
    )
    other = lax.ppermute(leaving, "seq", SWAP)
    local = call(chip_kernel, "chip", shape((CHIPS, 168, LANES), bf16), [], [held, other, small])
    gathered = same_core_all_to_all(local)
    states = shape((CHIPS, 160, LANES), bf16)
    entering = call(chain_kernel, "chain", states, [core], [gathered])
    carried = same_core_all_to_all(entering)
    scaled, inner = call(
        inside_kernel,
        "inside",
        (shape((TOK, WIDE), f32), three),
        [],
        [small, x, g],
        out_hbm=(0,),
        after=[entering],
        scratch=[pltpu.VMEM((TOK, WIDE), f32), dma],
        cost=(400_000_000, 4_000_000),
    )
    passed = call(pass_kernel, "pass", states, [], [carried, held, small], after=[inner])
    other_carried = lax.ppermute(passed, "seq", SWAP)
    turned = call(turn_kernel, "turn", shape((WIDE, TOK), bf16), [], [feats], cost=(0, 2_000_000))
    grads, head_grad, keep, send = call(
        last_kernel,
        "last",
        (
            shape((2 * TOK, 2 * LANES), bf16),
            shape((TOK, WIDE), bf16),
            shape((DP, HALF, LANES), f32),
            chunks,
        ),
        [core],
        [carried, other_carried, small, scaled, inner, turned, x, g, rate, skip],
        in_hbm=(3,),
        scratch=[
            pltpu.VMEM((TOK, WIDE), f32),
            pltpu.VMEM((LANES, WIDE), bf16),
            pltpu.VMEM((2 * TOK, 2 * WIDE), bf16),
            pltpu.VMEM((2 * TOK + 16, 2 * WIDE), bf16),
            pltpu.VMEM((WIDE, LANES), bf16),
            dma,
        ],
    )
    other = lax.ppermute(send, "seq", SWAP)
    input_grad, token = call(
        back_kernel,
        "back",
        (shape((TOK, WIDE), bf16), shape((8, LANES), f32)),
        [],
        [grads, weight],
        cost=(340_000_000, 3_000_000),
    )
    paired = call(join_kernel, "join", chunks, [], [keep, other, token])
    owned = lax.all_to_all(paired, "dp", 0, 0, tiled=True)
    owned = jnp.sum(owned.astype(f32), axis=0)
    parts = lax.all_gather(owned, "seq")
    bc_grad, dt_grad = call(
        finish_kernel, "finish", (shape((ROWS, LANES), f32), shape((HEADS, ROWS), f32)), [], [parts]
    )
    return input_grad[None], head_grad[None], bc_grad, dt_grad.T


def solution(mesh):
    in_specs = (
        P("dp", "seq", None),
        P("dp", "seq", None),
        P("dp", "seq", None),
        P("dp", None),
        P("dp", None),
        P(),
        P(),
        P(),
    )
    out_specs = (P("dp", "seq", None), P("dp", "seq", None), P("dp", None), P("dp", None))
    return jax.shard_map(body, mesh=mesh, in_specs=in_specs, out_specs=out_specs, check_vma=False)
```

```python
import math

import jax
import jax.numpy as jnp
from jax import lax
from jax.experimental import pallas as pl
from jax.experimental.pallas import tpu as pltpu
from jax.sharding import PartitionSpec as P

bf16, f32 = jnp.bfloat16, jnp.float32
highest = lax.Precision.HIGHEST

HEADS = 40
PAIRS = 20
TOK = 128
WIDE = 2560
ROWS = 80
DP = 32
SEQ = 16
CHIPS = 8
STATE = 64
HALF = 56
REST = 24
LANES = 128

NN = (((1,), (0,)), ((), ()))
NT = (((1,), (1,)), ((), ()))
TN = (((0,), (0,)), ((), ()))


def iota(shape, axis):
    return lax.broadcasted_iota(jnp.int32, shape, axis)


def ones_where(mask, dtype=f32):
    return jnp.where(mask, 1.0, 0.0).astype(dtype)


def mm(a, b, dims=NN):
    return lax.dot_general(a.astype(bf16), b.astype(bf16), dims, preferred_element_type=f32)


def high_low(value):
    high = value.astype(bf16)
    return high, (value - high.astype(f32)).astype(bf16)


def mm_exact(a, b, dims=NN):
    return lax.dot_general(a, b, dims, precision=highest, preferred_element_type=f32)


def head_of_lane(lane):
    return lane - jnp.where(lane >= 40, 40, 0) - jnp.where(lane >= 80, 40, 0)


def triple(row):
    place = ones_where(iota((HEADS, LANES), 0) == head_of_lane(iota((HEADS, LANES), 1)))
    return mm_exact(jnp.broadcast_to(row, (8, HEADS)), place)[0:1]


def split(value):
    lane = iota(value.shape, 1)
    first = value.astype(bf16).astype(f32)
    rest = value - first
    second = rest.astype(bf16).astype(f32)
    third = rest - second
    return jnp.where(lane < 40, first, jnp.where(lane < 80, second, third)).astype(bf16)


def spread_matrix(pair, pairs=1):
    k, lane = iota((LANES, LANES * pairs), 0), iota((LANES, LANES * pairs), 1)
    return ones_where(head_of_lane(k) == 2 * pair + (lane >> 6), bf16)


def gather_matrix(pair, pairs=1):
    lane, k = iota((LANES * pairs, LANES), 0), iota((LANES * pairs, LANES), 1)
    return ones_where(head_of_lane(k) == 2 * pair + (lane >> 6), bf16)


def pack_kernel(core_ref, bc_hbm, dt_hbm, out_ref, bc_ref, dt_ref, sems):
    copies = [
        pltpu.make_async_copy(bc_hbm, bc_ref, sems.at[0]),
        pltpu.make_async_copy(dt_hbm, dt_ref, sems.at[1]),
    ]
    for copy in copies:
        copy.start()
    for copy in copies:
        copy.wait()
    bc = bc_ref[...].astype(f32)
    row, lane = iota((HEADS, LANES), 0), iota((HEADS, LANES), 1)
    dt = [mm(dt_ref[...], ones_where(lane == row + 40 * k), TN) for k in range(3)]
    last = jnp.concatenate([dt[2][64:80], jnp.zeros((16, LANES), f32)], axis=0)
    packed = dt[0][0:32] + dt[1][32:64] + last
    second = jnp.concatenate([bc[HALF:ROWS], packed], axis=0)
    value = jnp.where(core_ref[0] == 0, bc[0:HALF], second).astype(bf16)
    for owner in range(DP):
        out_ref[owner] = value


def turn_kernel(feat_ref, out_ref):
    for part in range(PAIRS):
        rows = slice(LANES * part, LANES * part + LANES)
        out_ref[rows, :] = feat_ref[:, rows].T


def first_kernel(
    core_ref, mine_ref, other_ref, feat_hbm, x_ref, g_ref, bias_ref, rate_ref,
    weight_hbm, small_ref, held_ref, sent_ref, weight_ref, feat_ref, sems,
):
    fetch = pltpu.make_async_copy(feat_hbm, feat_ref, sems.at[0])
    fetch.start()
    lane16 = iota((16, LANES), 1)
    group = [
        ones_where((lane16 >= 40 * k) & (lane16 < 40 * k + 40), bf16) for k in range(3)
    ]

    def assemble(one_ref, two_ref):
        for owner in range(DP):
            base = ROWS * owner
            weight_ref[base : base + HALF, 0:LANES] = one_ref[owner]
            weight_ref[base + HALF : base + ROWS, 0:LANES] = two_ref[owner, 0:REST, :]
            low, high = two_ref[owner, 24:40, :], two_ref[owner, 40:56, :]
            weight_ref[base : base + 16, LANES:] = low * group[0]
            weight_ref[base + 16 : base + 32, LANES:] = high * group[0]
            weight_ref[base + 32 : base + 48, LANES:] = low * group[1]
            weight_ref[base + 48 : base + 64, LANES:] = high * group[1]
            weight_ref[base + 64 : base + 80, LANES:] = low * group[2]

    core = core_ref[0]

    @pl.when(core == 0)
    def _():
        assemble(mine_ref, other_ref)

    @pl.when(core != 0)
    def _():
        assemble(other_ref, mine_ref)

    store = pltpu.make_async_copy(weight_ref, weight_hbm, sems.at[1])
    store.start()
    fetch.wait()
    both = lax.dot_general(feat_ref[...], weight_ref[...], NN, preferred_element_type=f32)
    proj = both[:, 0:LANES]
    row, lane = iota((LANES, LANES), 0), iota((LANES, LANES), 1)
    head_row, head_lane = head_of_lane(row), head_of_lane(lane)
    fold = ones_where((head_row == head_lane) & (head_lane < HEADS))
    pre = mm_exact(both[:, LANES:], fold) + triple(bias_ref[...])
    step = jnp.maximum(pre, 0.0) + jnp.log1p(jnp.exp(-jnp.abs(pre)))
    cum = mm_exact(ones_where(row >= lane), -triple(rate_ref[...]) * step)
    small_ref[0] = proj
    small_ref[1] = pre
    small_ref[2] = cum
    total = cum[TOK - 1 : TOK]
    stacked = jnp.concatenate(
        [split(step * jnp.exp(total - cum)), split(jnp.exp(cum))], axis=0
    )
    turned_high, turned_low = high_low(proj.T)
    b_turned = jnp.concatenate([turned_high[0:STATE], turned_low[0:STATE]], axis=0)
    c_turned = jnp.concatenate([turned_high[STATE:], turned_low[STATE:]], axis=0)

    def product(turned, halves):
        value = mm(turned, halves[0])
        return value[0:STATE] + (value[STATE:] + mm(turned[0:STATE], halves[1]))

    for two in range(PAIRS // 2):
        cols = slice(256 * two, 256 * two + 256)
        rows = slice(16 * two, 16 * two + 16)
        wide = lax.dot_general(
            stacked, spread_matrix(2 * two, 2), NN, preferred_element_type=f32
        )
        onward = product(b_turned, high_low(x_ref[:, cols].astype(f32) * wide[0:TOK]))
        backward = product(c_turned, high_low(g_ref[:, cols].astype(f32) * wide[TOK:]))
        held_ref[:, rows, :] = to_chunks(jnp.where(core == 0, onward, backward))
        sent_ref[:, rows, :] = to_chunks(jnp.where(core == 0, backward, onward))
    for owner in range(CHIPS):
        sent_ref[owner, 160:168, :] = jnp.broadcast_to(total, (8, LANES))
    store.wait()


def to_chunks(value):
    parts = [value[:, LANES * k : LANES * k + LANES] for k in range(2)]
    return jnp.concatenate([part.reshape(CHIPS, 8, LANES) for part in parts], axis=1)


def chunk_factors(logs, two):
    wide = jnp.exp(
        lax.dot_general(logs, spread_matrix(2 * two, 2), NN, preferred_element_type=f32)
    )

    def factor(place):
        parts = [wide[place : place + 1, LANES * k : LANES * k + LANES] for k in range(2)]
        return jnp.concatenate([jnp.broadcast_to(part, (8, LANES)) for part in parts], axis=0)

    return factor


def chip_kernel(held_ref, other_ref, small_ref, out_ref):
    total_other = other_ref[0, 160:168, :]
    logs = split(jnp.concatenate([total_other, total_other], axis=0))
    for two in range(PAIRS // 2):
        rows = slice(16 * two, 16 * two + 16)
        factor = chunk_factors(logs, two)(0)
        for owner in range(CHIPS):
            value = other_ref[owner, rows, :] + held_ref[owner, rows, :] * factor
            out_ref[owner, rows, :] = value.astype(bf16)
    decay = split(total_other + small_ref[2, TOK - 1 : TOK, :])
    for owner in range(CHIPS):
        out_ref[owner, 160:168, :] = decay


def chain_kernel(core_ref, state_ref, out_ref):
    row16 = iota((16, LANES), 0)
    logs = jnp.zeros((16, LANES), f32)
    for place in range(CHIPS):
        line = state_ref[place, 160:168, :].astype(f32)
        logs = logs + jnp.where(row16 == place, jnp.concatenate([line, line], axis=0), 0.0)
    logs = logs.astype(bf16)
    forward = core_ref[0] == 0
    for two in range(PAIRS // 2):
        rows = slice(16 * two, 16 * two + 16)
        factor = chunk_factors(logs, two)
        values = [state_ref[place, rows, :].astype(f32) for place in range(CHIPS)]
        factors = [factor(place) for place in range(CHIPS)]
        ahead = [jnp.zeros((16, LANES), f32)]
        for place in range(CHIPS - 1):
            ahead.append(ahead[-1] * factors[place] + values[place])
        back = jnp.zeros((16, LANES), f32)
        for place in range(CHIPS - 1, -1, -1):
            out_ref[place, rows, :] = jnp.where(forward, ahead[place], back).astype(bf16)
            back = back * factors[place] + values[place]


def pass_kernel(carried_ref, held_ref, small_ref, after_ref, out_ref):
    logs = split(jnp.broadcast_to(small_ref[2, TOK - 1 : TOK, :], (16, LANES)))
    for two in range(PAIRS // 2):
        rows = slice(16 * two, 16 * two + 16)
        factor = chunk_factors(logs, two)(0)
        for owner in range(CHIPS):
            value = carried_ref[owner, rows, :].astype(f32) * factor + held_ref[owner, rows, :]
            out_ref[owner, rows, :] = value.astype(bf16)


def softplus(pre):
    return jnp.maximum(pre, 0.0) + jnp.log1p(jnp.exp(-jnp.abs(pre)))


def inside_kernel(
    small_ref, x_ref, g_ref, skip_ref, after_ref,
    base_hbm, sums_ref, lines_hbm, base_ref, lines_ref, sems,
):
    proj, cum = small_ref[0], small_ref[2]
    step = softplus(small_ref[1])
    row, lane = iota((LANES, LANES), 0), iota((LANES, LANES), 1)
    low = lane < STATE
    b_low = jnp.where(low, proj, 0.0)
    c_low = jnp.where(low, pltpu.roll(proj, STATE, 1), 0.0)
    meet = mm_exact(b_low, c_low, NT)
    causal = lane >= row
    cum_turned = cum.T
    lane_head = head_of_lane(lane)
    across = jnp.zeros((TOK, TOK), f32)
    own = jnp.zeros((TOK, LANES), f32)
    sums_ref[2] = jnp.zeros((LANES, TOK), f32)
    stacked = jnp.concatenate(
        [
            split(step),
            split(step * jnp.exp(cum[TOK - 1 : TOK] - cum)),
            split(jnp.exp(cum)),
            split(jnp.broadcast_to(triple(skip_ref[...]), (16, LANES))),
        ],
        axis=0,
    )
    first_half = ones_where(lane < 64, bf16)
    second_half = ones_where(lane >= 64, bf16)
    for pair in range(PAIRS):
        cols = slice(LANES * pair, LANES * pair + LANES)
        x, g = x_ref[:, cols], g_ref[:, cols]
        mixed, parts = [], []
        for which, half in enumerate((first_half, second_half)):
            head = 2 * pair + which
            g_half = g * half
            outer = lax.dot_general(x, g_half, NT, preferred_element_type=f32)
            gap = cum_turned[head : head + 1, :] - cum[:, head : head + 1]
            weight = jnp.exp(jnp.where(causal, gap, -1e30))
            step_col = step[:, head : head + 1]
            spot = outer * weight
            across = across + spot * step_col
            product = spot * meet
            own = jnp.where(lane_head == head, jnp.sum(product, axis=1, keepdims=True), own)
            sums_ref[2, head : head + 1, :] = jnp.sum(product * step_col, axis=0, keepdims=True)
            mixed.append((meet * weight).astype(bf16))
            parts.append(g_half)
        scaled = lax.dot_general(
            jnp.concatenate(mixed, axis=1), jnp.concatenate(parts, axis=0), NN,
            preferred_element_type=f32,
        )
        wide = lax.dot_general(stacked, spread_matrix(pair), NN, preferred_element_type=f32)
        x, g = x.astype(f32), g.astype(f32)
        base_ref[:, cols] = g * wide[3 * TOK : 3 * TOK + 1] + wide[0:TOK] * scaled
        high, low_part = high_low(
            jnp.concatenate([g * wide[2 * TOK : 3 * TOK], x * wide[TOK : 2 * TOK]], axis=0)
        )
        lines_ref[:, cols] = high
        lines_ref[:, WIDE + LANES * pair : WIDE + LANES * pair + LANES] = low_part
    sums_ref[0] = across
    sums_ref[1] = own
    copies = [
        pltpu.make_async_copy(base_ref, base_hbm, sems.at[0]),
        pltpu.make_async_copy(lines_ref, lines_hbm, sems.at[1]),
    ]
    for copy in copies:
        copy.start()
    for copy in copies:
        copy.wait()


def last_kernel(
    core_ref, carried_ref, other_ref, small_ref, base_hbm, inner_ref, lines_hbm, turned_ref,
    x_ref, g_ref, rate_ref,
    grads_ref, head_grad_ref, keep_ref, send_ref,
    base_ref, state_all, lines_all, terms_all, select_all, sems,
):
    fetch_base = pltpu.make_async_copy(base_hbm, base_ref, sems.at[0])
    fetch_base.start()
    fetch_lines = pltpu.make_async_copy(lines_hbm, lines_all, sems.at[1])
    fetch_lines.start()
    proj, pre, cum = small_ref[0], small_ref[1], small_ref[2]
    step = softplus(pre)
    total = cum[TOK - 1 : TOK]
    row, lane = iota((LANES, LANES), 0), iota((LANES, LANES), 1)
    low = lane < STATE
    proj_swapped = pltpu.roll(proj, STATE, 1)
    c_low = jnp.where(low, proj_swapped, 0.0)
    b_high = jnp.where(low, 0.0, proj_swapped)
    first_core = core_ref[0] == 0
    left = jnp.concatenate([c_low, b_high], axis=0)
    left = jnp.concatenate(high_low(left), axis=0)
    stacked = jnp.concatenate(
        [
            split(step * jnp.exp(total - cum)),
            split(jnp.exp(total - cum)),
            split(jnp.exp(cum)),
        ],
        axis=0,
    )

    def state_rows(chunk):
        parts = [chunk[:, 8 * k : 8 * k + 8, :].reshape(STATE, LANES) for k in range(2)]
        return jnp.concatenate(parts, axis=1)

    for two in range(PAIRS // 2):
        cols = slice(256 * two, 256 * two + 256)
        later_cols = slice(WIDE + 256 * two, WIDE + 256 * two + 256)
        rows = slice(16 * two, 16 * two + 16)
        mine = carried_ref[:, rows, :].astype(f32)
        other = other_ref[:, rows, :].astype(f32)
        state_in = state_rows(jnp.where(first_core, mine, other))
        state_grad = state_rows(jnp.where(first_core, other, mine))
        state_b = jnp.concatenate([state_in, state_grad], axis=0).astype(bf16)
        state_all[:, cols] = state_b
        select_all[cols, :] = gather_matrix(2 * two, 2)
        wide = lax.dot_general(
            stacked, spread_matrix(2 * two, 2), NN, preferred_element_type=f32
        )
        push_w, end_w, start_w = wide[0:TOK], wide[TOK : 2 * TOK], wide[2 * TOK :]
        x, g = x_ref[:, cols].astype(f32), g_ref[:, cols].astype(f32)
        weighted = g * start_w
        ending = x * end_w
        pushed = lax.dot_general(left, state_b, NN, preferred_element_type=f32)
        pushed = pushed[0 : 2 * TOK] + pushed[2 * TOK :]
        out, reach = pushed[0:TOK], pushed[TOK:]
        pairing = jnp.sum((state_in * state_grad).reshape(CHIPS, 8, 2 * LANES), axis=0)
        pairing = jnp.concatenate([pairing, jnp.zeros((8, 2 * LANES), f32)], axis=0)
        high, low_part = high_low(
            jnp.concatenate([weighted * out, ending * reach, pairing], axis=0)
        )
        terms_all[:, cols] = high
        terms_all[:, later_cols] = low_part
        if two == 0:
            fetch_base.wait()
        head_grad_ref[:, cols] = (base_ref[:, cols] + push_w * reach).astype(bf16)

    def both_parts(ref, right, dims):
        return lax.dot_general(
            ref[:, 0:WIDE], right, dims, preferred_element_type=f32
        ) + lax.dot_general(ref[:, WIDE:], right, dims, preferred_element_type=f32)

    fetch_lines.wait()
    crossed = both_parts(lines_all, state_all[...], NT)
    sums = both_parts(terms_all, select_all[...], NN)
    through, reached = sums[0:TOK], sums[TOK : 2 * TOK]
    paired = jnp.sum(sums[2 * TOK : 2 * TOK + 8], axis=0, keepdims=True)
    own = inner_ref[1]
    lane_head = head_of_lane(lane)
    later = mm_exact(inner_ref[2].T, ones_where((row == lane_head) & (row < HEADS)))
    decay_grad = (
        mm_exact(ones_where(lane >= row), later - step * own + through)
        + mm_exact(ones_where(lane < row), step * reached)
        + jnp.exp(total) * paired
    )
    step_grad = own + reached - triple(rate_ref[...]) * decay_grad
    pre_grad = step_grad * jax.nn.sigmoid(pre)
    pre_grad = jnp.where(lane < 3 * HEADS, pre_grad, 0.0)
    across = inner_ref[0]
    bc_grad = mm_exact(across, c_low) + mm_exact(across.T, b_high)
    bc_grad = bc_grad + jnp.where(
        low, pltpu.roll(crossed[TOK:], STATE, 1), pltpu.roll(crossed[0:TOK], STATE, 1)
    )
    grads = high_low(jnp.concatenate([bc_grad, pre_grad], axis=1))
    tall, flat = jnp.concatenate(grads, axis=0), jnp.concatenate(grads, axis=1)
    grads_ref[...] = tall
    lane32 = iota((32, LANES), 1)
    zeros = jnp.zeros((16, LANES), f32)
    for part in range(4):
        rows = slice(640 * part, 640 * part + 640)
        product = lax.dot_general(turned_ref[rows, :], flat, NN, preferred_element_type=f32)
        product = product[:, 0 : 2 * LANES] + product[:, 2 * LANES :]
        for inner in range(8):
            base = ROWS * inner
            dt = product[base : base + ROWS, LANES:]
            packed = jnp.where(
                lane32 < 40,
                dt[0:32],
                jnp.where(lane32 < 80, dt[32:64], jnp.concatenate([dt[64:80], zeros], axis=0)),
            )
            one = product[base : base + HALF, 0:LANES]
            two = jnp.concatenate([product[base + HALF : base + ROWS, 0:LANES], packed], axis=0)
            owner = 8 * part + inner
            keep_ref[owner] = jnp.where(first_core, one, two)
            send_ref[owner] = jnp.where(first_core, two, one).astype(bf16)


def back_kernel(grads_ref, weight_ref, input_grad_ref, token_ref):
    token_ref[...] = jnp.zeros_like(token_ref)
    tall = grads_ref[...]
    for part in range(10):
        cols = slice(256 * part, 256 * part + 256)
        product = lax.dot_general(tall, weight_ref[cols, :], NT, preferred_element_type=f32)
        input_grad_ref[:, cols] = (product[0:TOK] + product[TOK:]).astype(bf16)


def join_kernel(keep_ref, other_ref, token_ref, out_ref):
    for owner in range(DP):
        out_ref[owner] = (keep_ref[owner] + other_ref[owner].astype(f32)).astype(bf16)


def finish_kernel(parts_ref, bc_ref, dt_ref):
    one = parts_ref[0].astype(f32)
    two = parts_ref[1].astype(f32)
    for place in range(2, SEQ, 2):
        one = one + parts_ref[place].astype(f32)
        two = two + parts_ref[place + 1].astype(f32)
    scale = 1.0 / math.sqrt(SEQ * DP * TOK)
    bc = jnp.concatenate([one, two[0:REST]], axis=0) * scale
    bc_ref[...] = bc
    packed = two[REST:HALF] * scale
    head, lane = iota((HEADS, LANES), 0), iota((HEADS, LANES), 1)
    for k in range(3):
        rows = min(32, ROWS - 32 * k)
        dt_ref[:, 32 * k : 32 * k + rows] = mm_exact(
            ones_where(lane == head + 40 * k), packed[0:rows], NT
        )


def call(kernel, name, out_shape, scalars, arrays, in_hbm=(), out_hbm=(), after=(), **options):
    smem = pl.BlockSpec(memory_space=pltpu.SMEM)
    vmem = pl.BlockSpec(memory_space=pltpu.VMEM)
    hbm = pl.BlockSpec(memory_space=pltpu.HBM)
    flops, moved = options.pop("cost", (0, 0))
    several = isinstance(out_shape, tuple)
    if out_hbm:
        out_shape = tuple(
            pltpu.HBM(part.shape, part.dtype) if k in out_hbm else part
            for k, part in enumerate(out_shape)
        )
    arrays = [
        pltpu.with_memory_space_constraint(part, pltpu.HBM) if k in in_hbm else part
        for k, part in enumerate(arrays)
    ]
    out_specs = [hbm if k in out_hbm else vmem for k in range(len(out_shape))] if several else vmem
    return pl.pallas_call(
        kernel,
        name=name,
        out_shape=out_shape,
        in_specs=[smem] * len(scalars)
        + [hbm if k in in_hbm else vmem for k in range(len(arrays))]
        + [pl.BlockSpec(memory_space=pl.ANY)] * len(after),
        out_specs=tuple(out_specs) if several else out_specs,
        scratch_shapes=options.pop("scratch", ()),
        compiler_params=pltpu.CompilerParams(vmem_limit_bytes=40 << 20),
        cost_estimate=pl.CostEstimate(flops=flops, bytes_accessed=moved, transcendentals=0),
    )(*scalars, *arrays, *after)


def shape(dims, dtype):
    return jax.ShapeDtypeStruct(dims, dtype)


SWAP = [(place, place ^ 1) for place in range(SEQ)]
CORES = [[place for place in range(SEQ) if place % 2 == core] for core in range(2)]


def same_core_all_to_all(value):
    return lax.all_to_all(value, "seq", 0, 0, axis_index_groups=CORES, tiled=True)


def body(features, head_inputs, out_grad, bc_weight, dt_weight, dt_bias, decay_rate, skip_gain):
    core = (lax.axis_index("seq") & 1).astype(jnp.int32).reshape(1)
    feats, x, g = features[0], head_inputs[0], out_grad[0]
    bias, rate, skip = dt_bias[None], decay_rate[None], skip_gain[None]
    chunks = shape((DP, HALF, LANES), bf16)
    three = shape((3, TOK, LANES), f32)
    dma = pltpu.SemaphoreType.DMA

    sent = call(
        pack_kernel, "pack", chunks, [core], [bc_weight, dt_weight.T],
        in_hbm=(0, 1),
        scratch=[pltpu.VMEM((ROWS, LANES), bf16), pltpu.VMEM((HEADS, ROWS), bf16), dma((2,))],
    )
    mine = lax.all_to_all(sent, "dp", 0, 0, tiled=True)
    other = lax.ppermute(mine, "seq", SWAP)
    weight, small, held, leaving = call(
        first_kernel,
        "first",
        (
            shape((WIDE, 2 * LANES), bf16),
            three,
            shape((CHIPS, 160, LANES), f32),
            shape((CHIPS, 168, LANES), f32),
        ),
        [core],
        [mine, other, feats, x, g, bias, rate],
        in_hbm=(2,),
        out_hbm=(0,),
        scratch=[
            pltpu.VMEM((WIDE, 2 * LANES), bf16),
            pltpu.VMEM((TOK, WIDE), bf16),
            dma((2,)),
        ],
    )
    other = lax.ppermute(leaving, "seq", SWAP)
    local = call(chip_kernel, "chip", shape((CHIPS, 168, LANES), bf16), [], [held, other, small])
    gathered = same_core_all_to_all(local)
    states = shape((CHIPS, 160, LANES), bf16)
    entering = call(chain_kernel, "chain", states, [core], [gathered])
    carried = same_core_all_to_all(entering)
    base, inner, lines = call(
        inside_kernel,
        "inside",
        (shape((TOK, WIDE), f32), three, shape((2 * TOK, 2 * WIDE), bf16)),
        [],
        [small, x, g, skip],
        out_hbm=(0, 2),
        after=[entering],
        scratch=[
            pltpu.VMEM((TOK, WIDE), f32),
            pltpu.VMEM((2 * TOK, 2 * WIDE), bf16),
            dma((2,)),
        ],
        cost=(400_000_000, 4_000_000),
    )
    passed = call(pass_kernel, "pass", states, [], [carried, held, small], after=[inner])
    other_carried = lax.ppermute(passed, "seq", SWAP)
    turned = call(turn_kernel, "turn", shape((WIDE, TOK), bf16), [], [feats], cost=(0, 2_000_000))
    grads, head_grad, keep, send = call(
        last_kernel,
        "last",
        (
            shape((2 * TOK, 2 * LANES), bf16),
            shape((TOK, WIDE), bf16),
            shape((DP, HALF, LANES), f32),
            chunks,
        ),
        [core],
        [carried, other_carried, small, base, inner, lines, turned, x, g, rate],
        in_hbm=(3, 5),
        scratch=[
            pltpu.VMEM((TOK, WIDE), f32),
            pltpu.VMEM((LANES, WIDE), bf16),
            pltpu.VMEM((2 * TOK, 2 * WIDE), bf16),
            pltpu.VMEM((2 * TOK + 16, 2 * WIDE), bf16),
            pltpu.VMEM((WIDE, LANES), bf16),
            dma((2,)),
        ],
    )
    other = lax.ppermute(send, "seq", SWAP)
    input_grad, token = call(
        back_kernel,
        "back",
        (shape((TOK, WIDE), bf16), shape((8, LANES), f32)),
        [],
        [grads, weight],
        cost=(340_000_000, 3_000_000),
    )
    paired = call(join_kernel, "join", chunks, [], [keep, other, token])
    owned = lax.all_to_all(paired, "dp", 0, 0, tiled=True)
    owned = jnp.sum(owned.astype(f32), axis=0)
    parts = lax.all_gather(owned, "seq")
    bc_grad, dt_grad = call(
        finish_kernel, "finish", (shape((ROWS, LANES), f32), shape((HEADS, ROWS), f32)), [], [parts]
    )
    return input_grad[None], head_grad[None], bc_grad, dt_grad.T


def solution(mesh):
    in_specs = (
        P("dp", "seq", None),
        P("dp", "seq", None),
        P("dp", "seq", None),
        P("dp", None),
        P("dp", None),
        P(),
        P(),
        P(),
    )
    out_specs = (P("dp", "seq", None), P("dp", "seq", None), P("dp", None), P("dp", None))
    return jax.shard_map(body, mesh=mesh, in_specs=in_specs, out_specs=out_specs, check_vma=False)
```
